32 devices in a mesh: row: 8 (over z, y), col: 4 (over x, core).
Axes of the slice: x: 2, y: 2, z: 4, core: 2. Of those that a mesh axis runs over, the one named last changes fastest.
Arguments:
- tokens: bfloat16 [16, 2048, 768], P('row', 'col'), may hold values from -6 to 6
- segment_ids: int32 [16, 2048], P('row', 'col'), may hold values from 0 to 1, never falling along the last dimension, each value on 1 to 2000 neighbouring positions
- in_weight: bfloat16 [768, 2304], P('row', 'col'), may hold values from -0.21875 to 0.21875
- in_bias: bfloat16 [2304], replicated, may hold values from -3 to 3
- mix_weight: bfloat16 [768, 768], P('row', 'col'), may hold values from -1.5 to 1.5
- mix_bias: bfloat16 [768], replicated, may hold values from -3 to 3
- first_gain: bfloat16 [768], replicated, may hold values from 0.25 to 1.75
- first_shift: bfloat16 [768], replicated, may hold values from -3 to 3
- up_weight: bfloat16 [768, 3072], P('row', 'col'), may hold values from -0.21875 to 0.21875
- up_bias: bfloat16 [3072], replicated, may hold values from -3 to 3
- down_weight: bfloat16 [3072, 768], P('row', 'col'), may hold values from -0.109375 to 0.109375
- down_bias: bfloat16 [768], replicated, may hold values from -3 to 3
- second_gain: bfloat16 [768], replicated, may hold values from 0.25 to 1.75
- second_shift: bfloat16 [768], replicated, may hold values from -3 to 3
- cotangent: float32 [16, 2048, 768], P('row', 'col'), may hold values from -6 to 6
Outputs:
- layer_out: bfloat16 [16, 2048, 768], P('row', 'col')
- tokens_grad: float32 [16, 2048, 768], P('row', 'col')
- in_weight_grad: float32 [768, 2304], P('row', 'col')
- in_bias_grad: float32 [2304], replicated
- mix_weight_grad: float32 [768, 768], P('row', 'col')
- mix_bias_grad: float32 [768], replicated
- first_gain_grad: float32 [768], replicated
- first_shift_grad: float32 [768], replicated
- up_weight_grad: float32 [768, 3072], P('row', 'col')
- up_bias_grad: float32 [3072], replicated
- down_weight_grad: float32 [3072, 768], P('row', 'col')
- down_bias_grad: float32 [768], replicated
- second_gain_grad: float32 [768], replicated
- second_shift_grad: float32 [768], replicated
The draws below stay inside these ranges and needn't reach their ends.
Inputs may be any that keep to these rules, and one draw needn't show every extreme that they name: `segment_ids`: in each sequence 2 documents numbered from 0 in order of position; each covers 1 to 2000 consecutive positions.
All inputs are finite; a program needn't handle non-finite values.
Results may differ from the reference program's by a relative error of at most 0.019.
Values may be sent and summed in bfloat16 or wider, within the bound.
A program may use at most 256 MiB of HBM per device.

```python
import math
import jax
import jax.numpy as jnp
import numpy as np
from jax import lax

D = 768
FF = 3072
HEADS = 12
HEAD_DIM = 64
SEQ_DEV = 512
DOC_MAX = 2000
LEN = 2048
NSEQ = 16
DOCS = 2


def steps_of(stream_key, extent, split, least, largest):
    def one(dim, shards_of):
        draws = jax.random.uniform(jax.random.fold_in(jax.random.fold_in(stream_key, 6), dim), (shards_of,), jnp.float32, least / len(split), largest / len(split))
        return jnp.repeat(jnp.exp(draws), extent[dim] // shards_of).reshape((-1,) + (1,) * (len(extent) - dim - 1))

    loudness = one(*split[0])
    for cut in split[1:]:
        loudness = loudness * one(*cut)
    return loudness


def length_profile(amount, total, reach, skew):
    loads = [(1 << 20) // math.isqrt(grade ** skew) + 1 for grade in range(2, amount + 1)]
    rest, counts = total - reach - (amount - 1), [1] * (amount - 1)
    while rest > 0:
        candidates = [i for i in range(amount - 1) if counts[i] < reach]
        whole, left = sum([loads[i] for i in candidates]), rest
        for i in candidates:
            more = min(reach - counts[i], max(1, left * loads[i] // whole), rest)
            counts[i] = counts[i] + more
            rest = rest - more
    return np.array([reach] + counts)


def ragged_sizes(rng, count, total, most, skew):
    if count == 2:
        one = jax.random.randint(rng, (), max(1, total - most), min(most, total - 1) + 1)
        return jnp.stack([one, total - one])
    lengths = jnp.asarray(length_profile(count, total, most, skew), jnp.int32)
    twos = (count - 1) // 2
    giver, sink = lengths[1:1 + 2 * twos:2], lengths[2:2 + 2 * twos:2]
    slack = jnp.minimum(giver - 1, most - sink)
    moved = jax.random.randint(jax.random.fold_in(rng, 1), (twos,), 0, 1 << 20) % (slack + 1)
    lengths = lengths.at[1:1 + 2 * twos:2].set(giver - moved).at[2:2 + 2 * twos:2].set(sink + moved)
    return lengths[jax.random.permutation(jax.random.fold_in(rng, 2), count)]


def normal_values(own_key, shape, deviation, most, split=(), kind=jnp.bfloat16):
    loudness = steps_of(own_key, shape, split, -0.22, 0.18) if split else 1.0
    entries = jax.random.normal(own_key, shape, jnp.float32) * deviation * loudness
    return jnp.minimum(jnp.maximum(entries, -most), most).astype(kind)


def setup_inputs(seed: int = 0) -> dict:
    keys = jax.random.split(jax.random.key(seed), 16)
    return {
        "tokens": normal_values(keys[0], (NSEQ, LEN, D), 1.0, 6.0, ((0, 8), (1, 4))),
        "segment_ids": jax.vmap(lambda own: jnp.searchsorted(jnp.cumsum(ragged_sizes(own, DOCS, LEN, DOC_MAX, 0)), jnp.arange(LEN), side="right"))(jax.random.split(keys[1], NSEQ)).reshape((NSEQ, LEN)).astype(jnp.int32),
        "in_weight": normal_values(keys[2], (D, 3 * D), D ** -0.5, 0.21875, ((0, 8), (1, 4))),
        "in_bias": normal_values(keys[3], (3 * D,), 0.5, 3.0),
        "mix_weight": normal_values(keys[4], (D, D), 16 ** -0.5, 1.5, ((0, 8), (1, 4))),
        "mix_bias": normal_values(keys[5], (D,), 0.5, 3.0),
        "first_gain": jnp.clip(1.0 + 0.15 * jax.random.normal(keys[6], (D,), jnp.float32), 0.25, 1.75).astype(jnp.bfloat16),
        "first_shift": normal_values(keys[7], (D,), 0.5, 3.0),
        "up_weight": normal_values(keys[8], (D, FF), D ** -0.5, 0.21875, ((0, 8), (1, 4))),
        "up_bias": normal_values(keys[9], (FF,), 0.5, 3.0),
        "down_weight": normal_values(keys[10], (FF, D), FF ** -0.5, 0.109375, ((0, 8), (1, 4))),
        "down_bias": normal_values(keys[11], (D,), 0.5, 3.0),
        "second_gain": jnp.clip(1.0 + 0.15 * jax.random.normal(keys[12], (D,), jnp.float32), 0.25, 1.75).astype(jnp.bfloat16),
        "second_shift": normal_values(keys[13], (D,), 0.5, 3.0),
        "cotangent": normal_values(keys[14], (NSEQ, LEN, D), 1.0, 6.0, ((0, 8), (1, 4)), jnp.float32),
    }


@jax.custom_vjp
def low(v):
    return lax.optimization_barrier(v.astype(jnp.bfloat16)).astype(jnp.float32)

@jax.custom_vjp
def low_back(v):
    return v

def low_keep(v):
    return (low(v), None)

def low_pass(kept, grad):
    return (grad,)

def back_keep(v):
    return (v, None)

def back_low(kept, grad):
    return (low(grad),)
low.defvjp(low_keep, low_pass)
low_back.defvjp(back_keep, back_low)
EPSILON = 1e-05
FLOOR = 4.0
PRECISE = lax.Precision.HIGHEST

def product(first, second):
    return jnp.dot(first, second, precision=PRECISE, preferred_element_type=jnp.float32)

def layer_norm(values, gain_vec, shift_vec):
    center = values - lax.optimization_barrier(jnp.mean(values, axis=-1, keepdims=True))
    spread = lax.optimization_barrier(jnp.mean(center * center, axis=-1, keepdims=True))
    return center * lax.rsqrt(spread + EPSILON) * gain_vec + shift_vec

def doc_layout(doc_ids):
    indices = jnp.arange(LEN, dtype=jnp.int32)
    fresh_doc = jnp.concatenate([jnp.ones((1,), jnp.bool_), doc_ids[1:] != doc_ids[:-1]])
    doc_starts = lax.cummax(jnp.where(fresh_doc, indices, 0), axis=0)
    positions = indices - doc_starts
    blocked = doc_ids.reshape(LEN // SEQ_DEV, SEQ_DEV)
    before = jnp.concatenate([jnp.full((1,), -1, jnp.int32), blocked[:-1, -1]])
    carry_mask = blocked == before[:, None]
    last_mask = blocked == blocked[:, -1:]
    keep_flag = (blocked[:, 0] == blocked[:, -1]) & (blocked[:, 0] == before)
    return (positions, blocked, carry_mask, last_mask, keep_flag)

def features(pre_act, cosine, sine_part):
    active = jax.nn.relu(pre_act)
    return low(jnp.concatenate([active * cosine, active * sine_part], axis=-1))

def attend_block(carried, inputs):
    states, totals = carried
    query_feats, key_feats, values, doc_ids, carry_mask, last_mask, keep_flag = inputs
    indices = jnp.arange(SEQ_DEV, dtype=jnp.int32)
    allowed = ((doc_ids[:, None] == doc_ids[None, :]) & (indices[None, :] <= indices[:, None])).astype(jnp.float32)
    scores = low_back(jnp.einsum('ihf,jhf->hij', query_feats, key_feats, precision=PRECISE) * allowed[None])
    carry_float = carry_mask.astype(jnp.float32)[:, None]
    numerator = jnp.einsum('hij,jhd->ihd', low(scores), values, precision=PRECISE)
    numerator = numerator + carry_float[:, :, None] * jnp.einsum('ihf,hfd->ihd', query_feats, states, precision=PRECISE)
    numerator = low_back(numerator)
    denominator = lax.optimization_barrier(jnp.sum(scores, axis=-1)).T + carry_float * jnp.einsum('ihf,hf->ih', query_feats, totals, precision=PRECISE)
    attended = numerator / jnp.maximum(denominator, FLOOR)[:, :, None]
    last_float = last_mask.astype(jnp.float32)[:, None, None]
    keep_float = keep_flag.astype(jnp.float32)
    key_last = key_feats * last_float
    states = keep_float * states + jnp.einsum('jhf,jhd->hfd', key_last, values, precision=PRECISE)
    totals = keep_float * totals + lax.optimization_barrier(jnp.sum(key_last, axis=0))
    return ((states, totals), attended)

def attend(projected, layout):
    positions, blocked, carry_mask, last_mask, keep_flag = layout
    angles = positions.astype(jnp.float32) * (math.pi / (2.0 * DOC_MAX))
    cosine = jnp.cos(angles)[:, None, None]
    sine_part = jnp.sin(angles)[:, None, None]
    query_pre = projected[:, :D].reshape(LEN, HEADS, HEAD_DIM)
    key_pre = projected[:, D:2 * D].reshape(LEN, HEADS, HEAD_DIM)
    values = low(projected[:, 2 * D:].reshape(LEN, HEADS, HEAD_DIM))
    block_count = LEN // SEQ_DEV
    query_feats = features(query_pre, cosine, sine_part).reshape(block_count, SEQ_DEV, HEADS, 2 * HEAD_DIM)
    key_feats = features(key_pre, cosine, sine_part).reshape(block_count, SEQ_DEV, HEADS, 2 * HEAD_DIM)
    value_blocks = values.reshape(block_count, SEQ_DEV, HEADS, HEAD_DIM)
    initial = (jnp.zeros((HEADS, 2 * HEAD_DIM, HEAD_DIM), jnp.float32), jnp.zeros((HEADS, 2 * HEAD_DIM), jnp.float32))
    final_carry, attended = lax.scan(jax.checkpoint(attend_block), initial, (query_feats, key_feats, value_blocks, blocked, carry_mask, last_mask, keep_flag))
    return attended.reshape(LEN, D)

def layer(params, inputs, layout):
    in_weight, in_bias, mix_weight, mix_bias, first_gain, first_shift, up_weight, up_bias, down_weight, down_bias, second_gain, second_shift = params
    projected = low_back(product(inputs, in_weight) + in_bias)
    attended = attend(projected, layout)
    mixed = low_back(product(low(attended), mix_weight) + mix_bias)
    hidden = layer_norm(inputs + mixed, first_gain, first_shift)
    up_proj = low_back(product(low(hidden), up_weight) + up_bias)
    activated = low(jax.nn.gelu(up_proj, approximate=False))
    down_proj = low_back(product(activated, down_weight) + down_bias)
    return layer_norm(hidden + down_proj, second_gain, second_shift)

def reference(tokens, segment_ids, in_weight, in_bias, mix_weight, mix_bias, first_gain, first_shift, up_weight, up_bias, down_weight, down_bias, second_gain, second_shift, cotangent):
    params = tuple((argument.astype(jnp.float32) for argument in (in_weight, in_bias, mix_weight, mix_bias, first_gain, first_shift, up_weight, up_bias, down_weight, down_bias, second_gain, second_shift)))

    def one_sequence(summed, inputs):
        seq_tokens, seq_ids, seq_cotangent = inputs
        layout = doc_layout(seq_ids)

        def run_layer(param_set, values):
            return layer(param_set, values, layout)
        result, pullback = jax.vjp(run_layer, params, seq_tokens.astype(jnp.float32))
        param_grads, token_grads = pullback(seq_cotangent.astype(jnp.float32))
        summed = jax.tree.map(lambda total_sum, new_term: total_sum + new_term, summed, param_grads)
        return (summed, (result.astype(jnp.bfloat16), token_grads))
    zero_grads = jax.tree.map(jnp.zeros_like, params)
    summed, outputs = lax.scan(one_sequence, zero_grads, (tokens, segment_ids, cotangent))
    return (outputs[0], outputs[1], summed[0], summed[1], summed[2], summed[3], summed[4], summed[5], summed[6], summed[7], summed[8], summed[9], summed[10], summed[11])
```

```python
import functools
import math

import jax
import jax.numpy as jnp
from jax import lax
from jax.experimental import pallas as pl
from jax.experimental.pallas import tpu as pltpu
from jax.sharding import PartitionSpec as P

HEADS = 12
HEAD_DIM = 64
DOC_MAX = 2000
EPSILON = 1e-05
FLOOR = 4.0
OMEGA = math.pi / (2.0 * DOC_MAX)
MESH = pl.DeviceIdType.MESH
F32 = jnp.float32
BF16 = jnp.bfloat16
VMEM_LIMIT = 67_043_328

NN = (((1,), (0,)), ((), ()))
NT = (((1,), (1,)), ((), ()))
TN = (((0,), (0,)), ((), ()))


def dot(first, second, dims=NN):
    return lax.dot_general(first, second, dims, preferred_element_type=F32)


class Layout:
    def __init__(self, rows, cols):
        self.R, self.C = rows, cols
        self.Z = 4 if rows % 4 == 0 else rows
        self.Y = rows // self.Z
        self.K = 2
        self.X = cols // 2
        self.hops = (self.Z - 1) + (self.Y - 1) + (self.X - 1) + 1


class Place:
    def __init__(self, lay):
        self.lay = lay
        self.r = lax.axis_index("row")
        self.c = lax.axis_index("col")
        self.z, self.y = self.r // lay.Y, self.r % lay.Y
        self.x, self.k = self.c // 2, self.c % 2

    def at(self, z=None, y=None, x=None, k=None):
        z = self.z if z is None else z
        y = self.y if y is None else y
        x = self.x if x is None else x
        k = self.k if k is None else k
        return {"row": z * self.lay.Y + y, "col": x * 2 + k}

    def zs(self):
        return [lax.rem(self.z + d, self.lay.Z) for d in range(1, self.lay.Z)]

    def ys(self):
        return [lax.rem(self.y + d, self.lay.Y) for d in range(1, self.lay.Y)]

    def xs(self):
        return [lax.rem(self.x + d, self.lay.X) for d in range(1, self.lay.X)]

    def ring(self, step):
        return {"row": self.r, "col": lax.rem(self.c + step + self.lay.C, self.lay.C)}

    def barrier(self):
        peers = [self.at(z=z) for z in self.zs()] + [self.at(y=y) for y in self.ys()]
        peers += [self.at(x=x) for x in self.xs()] + [self.at(k=1 - self.k)]
        peers += [self.ring(1), self.ring(-1)]
        sem = pltpu.get_barrier_semaphore()
        for peer in peers:
            pl.semaphore_signal(sem, inc=1, device_id=peer, device_id_type=MESH)
        pl.semaphore_wait(sem, len(peers))


def remote(src, dst, send, recv, device):
    return pltpu.make_async_remote_copy(
        src_ref=src, dst_ref=dst, send_sem=send, recv_sem=recv, device_id=device, device_id_type=MESH
    )


class Gather:
    def __init__(self, place, shard, whole, r0, n, y_first, send, recv, base):
        self.p, self.shard, self.whole = place, shard, whole
        self.rows = pl.ds(r0, n)
        self.y_first = y_first
        self.send, self.recv, self.base = send, recv, base

    def stage(self, number):
        p, g, rows, lay = self.p, self.whole, self.rows, self.p.lay
        first, copies = self.base, []
        if number == 0:
            for z in p.zs():
                copies.append((self.shard.at[rows], g.at[p.x, p.k, p.z, p.y, rows], p.at(z=z)))
        else:
            first += lay.Z - 1
            along_y = (number == 1) == self.y_first
            if number == 3:
                part = g.at[:, p.k, :, :, rows]
                copies.append((part, part, p.at(k=1 - p.k)))
                first += lay.Y - 1 + lay.X - 1
            else:
                if number == 2:
                    first += (lay.Y - 1) if self.y_first else (lay.X - 1)
                    part = g.at[:, p.k, :, p.y, rows] if along_y else g.at[p.x, p.k, :, :, rows]
                else:
                    part = g.at[p.x, p.k, :, p.y, rows]
                for peer in [p.at(y=y) for y in p.ys()] if along_y else [p.at(x=x) for x in p.xs()]:
                    copies.append((part, part, peer))
        return [
            remote(src, dst, self.send.at[first + i], self.recv.at[first + i], device)
            for i, (src, dst, device) in enumerate(copies)
        ]

    def start(self, number):
        for copy in self.stage(number):
            copy.start()

    def arrive(self, number):
        for copy in self.stage(number):
            copy.wait_recv()

    def advance(self, number):
        self.arrive(number - 1)
        self.start(number)

    def sent(self):
        for number in range(4):
            for copy in self.stage(number):
                copy.wait_send()


def pieces(rows, count):
    tiles, many = rows // 16, 2 * count
    many = min(many, tiles)
    cuts = [(tiles * i + many - 1) // many for i in range(many + 1)]
    return [(cuts[i] * 16, (cuts[i + 1] - cuts[i]) * 16, i % 2 == 1) for i in range(many)]


def lane_half(head):
    lane = lax.broadcasted_iota(jnp.int32, (1, 128), 1)
    return ((lane < 64) if head == 0 else (lane >= 64)).astype(F32)


def same_head():
    row = lax.broadcasted_iota(jnp.int32, (128, 128), 0)
    lane = lax.broadcasted_iota(jnp.int32, (128, 128), 1)
    return ((row < 64) == (lane < 64)).astype(F32)


def seq_masks(ids_ref, prev_ref, seq, length, has_prev):
    row = ids_ref[seq : seq + 1, :].astype(F32)
    column = jnp.transpose(jnp.broadcast_to(row, (128, length)))
    lane = lax.broadcasted_iota(jnp.int32, (1, length), 1)
    first = jnp.sum(jnp.where(lane == 0, row, 0.0), axis=1, keepdims=True)
    last = jnp.sum(jnp.where(lane == length - 1, row, 0.0), axis=1, keepdims=True)
    before = prev_ref[seq : seq + 1, :].astype(F32)
    before = jnp.sum(jnp.where(lane == length - 1, before, 0.0), axis=1, keepdims=True)
    before = jnp.where(has_prev, before, -1.0)
    carry = (column == before).astype(F32)
    last_mask = (column == last).astype(F32)
    passes = ((first == last) & (first == before)).astype(F32)
    return row, column, carry, last_mask, passes


def angle_tables(length):
    column = lax.broadcasted_iota(jnp.int32, (length, 128), 0).astype(F32) * OMEGA
    row = lax.broadcasted_iota(jnp.int32, (1, length), 1).astype(F32) * OMEGA
    return jnp.cos(column), jnp.sin(column), jnp.cos(row), jnp.sin(row)


def edge_angles(cosine, sine, length):
    turn_c, turn_s = math.cos(OMEGA * length), math.sin(OMEGA * length)
    return cosine * turn_c + sine * turn_s, sine * turn_c - cosine * turn_s


def unpack_state(block):
    low, high = lane_half(0), lane_half(1)
    out = []
    for half in (0, 1):
        part = block[0:64, half * 128 : half * 128 + 128].astype(F32)
        out.append(jnp.concatenate([part * low, part * high], axis=0))
    return out


def pack_state(square):
    square = square * same_head()
    return square[0:64] + square[64:128]


def unslot(whole, flat, lay, a, b, transposed):
    for c in range(lay.C):
        if transposed:
            for r in range(lay.R):
                flat[c * a : (c + 1) * a, r * b : (r + 1) * b] = whole[
                    c // 2, c % 2, r // lay.Y, r % lay.Y
                ]
        else:
            for z in range(lay.Z):
                for y in range(lay.Y):
                    r = z * lay.Y + y
                    flat[r * a : (r + 1) * a, c * b : (c + 1) * b] = whole[c // 2, c % 2, z, y]


def forward_kernel(
    lay, seqs, length, cuts,
    tokens, ids, bias, in_s, mix_s, up_s, down_s,
    q_out, k_out, v_out, att, den, carry, prev, full_in, g_mix, g_up, g_down,
    g_in, mask, tab, out_state, flags,
    send, recv, misc_send, misc_recv, local,
):
    p = Place(lay)
    pairs = q_out.shape[1] // 128
    width = q_out.shape[1]
    total = seqs * pairs
    p.barrier()
    flows = []
    base = 0
    groups = []
    for shard, whole, parts in zip(
        (in_s, mix_s, up_s, down_s), (g_in, g_mix, g_up, g_down), cuts, strict=True
    ):
        group = []
        for r0, n, y_first in parts:
            group.append(Gather(p, shard, whole, r0, n, y_first, send, recv, base))
            base += lay.hops
        groups.append(group)
        flows += group
    own = [
        pltpu.make_async_copy(shard, whole.at[p.x, p.k, p.z, p.y], local.at[i])
        for i, (shard, whole) in enumerate(
            zip((in_s, mix_s, up_s, down_s), (g_in, g_mix, g_up, g_down), strict=True)
        )
    ]
    for copy in own:
        copy.start()
    ring_ids = remote(ids, prev, misc_send.at[0], misc_recv.at[0], p.ring(1))
    ring_ids.start()
    for flow in flows:
        flow.start(0)
    for copy in own:
        copy.wait()
    for flow in groups[0]:
        flow.advance(1)

    cos_a, sin_a, cos_r, sin_r = angle_tables(length)
    cos_e, sin_e = edge_angles(cos_a, sin_a, length)
    ring_ids.wait_recv()
    for s in range(seqs):
        row, column, carried, last_mask, passes = seq_masks(ids, prev, s, length, p.c > 0)
        at_i = lax.broadcasted_iota(jnp.int32, (length, length), 0)
        at_j = lax.broadcasted_iota(jnp.int32, (length, length), 1)
        allowed = (column[:, 0:1] == row) & (at_j <= at_i)
        mask[s] = jnp.where(allowed, cos_a[:, 0:1] * cos_r + sin_a[:, 0:1] * sin_r, 0.0)
        tab[s, 0] = cos_a * carried
        tab[s, 1] = sin_a * carried
        tab[s, 2] = cos_e * last_mask
        tab[s, 3] = sin_e * last_mask
        flags[s] = jnp.broadcast_to(passes, (8, 256))

    for number in (2, 3):
        for flow in groups[0]:
            flow.advance(number)
    for flow in groups[0]:
        flow.arrive(3)
    unslot(g_in, full_in, lay, in_s.shape[0], in_s.shape[1], False)

    blocks = width // 256
    half = tokens.shape[0] // 2

    def project(target, start, relu):
        def column_block(j, _):
            lanes = pl.ds(pl.multiple_of(j * 256, 256), 256)
            source = pl.ds(pl.multiple_of(start + j * 256, 256), 256)
            for m in range(2):
                out = dot(tokens[m * half : (m + 1) * half, :], full_in[:, source]) + bias[:, source]
                if relu:
                    out = jnp.maximum(out, 0.0)
                target[m * half : (m + 1) * half, lanes] = out.astype(BF16)
            return 0

        lax.fori_loop(0, blocks, column_block, 0)

    project(q_out, 0, True)
    project(k_out, width, True)
    project(v_out, 2 * width, False)

    def where(it):
        s, pair = it // pairs, it % pairs
        return s, pl.ds(pl.multiple_of(s * length, length), length), pl.ds(pl.multiple_of(pair * 128, 128), 128)

    def local_state(it, _):
        s, rows, lanes = where(it)
        keys, values = k_out[rows, lanes], v_out[rows, lanes].astype(F32)
        scaled = jnp.concatenate([values * tab[s, 2], values * tab[s, 3]], axis=1).astype(BF16)
        state = dot(keys, scaled, TN)
        wide = keys.astype(F32)
        for part in (0, 1):
            packed = pack_state(state[:, part * 128 : part * 128 + 128])
            out_state[it, 0:64, part * 128 : part * 128 + 128] = packed.astype(BF16)
            total_row = jnp.sum(wide * tab[s, 2 + part], axis=0, keepdims=True)
            out_state[it, 64:80, part * 128 : part * 128 + 128] = jnp.broadcast_to(total_row, (16, 128)).astype(BF16)
        return 0

    lax.fori_loop(0, total, local_state, 0)

    def chain_copy():
        return remote(out_state, carry, misc_send.at[1], misc_recv.at[1], p.ring(1))

    turn_c, turn_s = math.cos(OMEGA * length), math.sin(OMEGA * length)

    def hand_on():
        def one(it, _):
            came = carry[it].astype(F32)
            came_c, came_s = came[:, 0:128], came[:, 128:256]
            turned = jnp.concatenate(
                [came_c * turn_c + came_s * turn_s, came_s * turn_c - came_c * turn_s], axis=1
            )
            state = out_state[it].astype(F32) + flags[it // pairs, 0:1, :] * turned
            out_state[it] = state.astype(BF16)
            return 0

        lax.fori_loop(0, total, one, 0)

    def chain_step():
        @pl.when(p.c == 0)
        def _():
            carry[...] = jnp.zeros_like(carry)

        @pl.when(p.c > 0)
        def _():
            chain_copy().wait_recv()
            hand_on()

        @pl.when(p.c < lay.C - 1)
        def _():
            chain_copy().start()

    def fine(number):
        return [functools.partial(f.advance, number) for f in groups[1]], [
            functools.partial(f.advance, number) for f in groups[2]
        ], [functools.partial(f.advance, number) for f in groups[3]]

    m1, u1, d1 = fine(1)
    m2, u2, d2 = fine(2)
    m3, u3, d3 = fine(3)
    thunks = m1 + u1 + m2 + m3 + d1 + u2 + d2 + u3 + d3
    step_block = 256 if length % 256 == 0 else length

    def local_attention(it, _):
        @pl.when(it == (p.c * total) // lay.C)
        def _():
            chain_step()

        for n, thunk in enumerate(thunks):

            @pl.when(it == (n * total) // len(thunks))
            def _(thunk=thunk):
                thunk()

        s, rows, lanes = where(it)
        low, high = lane_half(0), lane_half(1)
        queries, keys, values = q_out[rows, lanes], k_out[rows, lanes], v_out[rows, lanes]
        for b in range(length // step_block):
            lo, reach = b * step_block, (b + 1) * step_block
            q = queries[lo:reach]
            numer = jnp.zeros((step_block, 128), F32)
            denom = jnp.zeros((step_block, 128), F32)
            for side in (low, high):
                only = side.astype(BF16)
                scores = dot(q, keys[:reach] * only, NT) * mask[s, lo:reach, 0:reach]
                numer = numer + dot(scores.astype(BF16), values[:reach] * only)
                denom = denom + jnp.sum(scores, axis=1, keepdims=True) * side
            here = pl.ds(pl.multiple_of(s * length + lo, step_block), step_block)
            att[here, lanes] = numer
            den[here, lanes] = denom
        return 0

    lax.fori_loop(0, total, local_attention, 0)

    square = same_head()

    def finish(it, _):
        s, rows, lanes = where(it)
        state_c, state_s = unpack_state(carry[it])
        totals = []
        for part in (0, 1):
            line = carry[it, 64:80, part * 128 : part * 128 + 128].astype(F32)[0:1]
            totals.append(jnp.transpose(jnp.broadcast_to(line, (128, 128))) * square)
        wide = jnp.concatenate([state_c, state_s, totals[0], totals[1]], axis=1).astype(BF16)
        reach = dot(q_out[rows, lanes], wide)
        c_i, s_i = tab[s, 0], tab[s, 1]
        numer = att[rows, lanes] + c_i * reach[:, 0:128] + s_i * reach[:, 128:256]
        denom = den[rows, lanes] + c_i * reach[:, 256:384] + s_i * reach[:, 384:512]
        den[rows, lanes] = denom
        att[rows, lanes] = numer / jnp.maximum(denom, FLOOR)
        return 0

    lax.fori_loop(0, total, finish, 0)

    for flow in flows[len(groups[0]) :]:
        flow.arrive(3)
    for flow in flows:
        flow.sent()
    ring_ids.wait_send()

    @pl.when(p.c < lay.C - 1)
    def _():
        chain_copy().wait_send()


def forward(lay, tokens, ids, bias, shards):
    seqs, length = ids.shape
    rows, width = tokens.shape
    total = seqs * (width // 128)
    cuts = [pieces(s.shape[0], n) for s, n in zip(shards, (3, 1, 1, 1), strict=True)]
    cuts = tuple(cuts)
    flows = sum(len(c) for c in cuts)
    vmem, anyspace = pl.BlockSpec(memory_space=pltpu.VMEM), pl.BlockSpec(memory_space=pl.ANY)
    slots = [(lay.X, 2, lay.Z, lay.Y) + s.shape for s in shards]
    shape = jax.ShapeDtypeStruct
    outs = (
        [shape((rows, width), BF16)] * 3
        + [shape((rows, width), F32)] * 2
        + [shape((total, 80, 256), BF16), shape(ids.shape, jnp.int32), shape((width, 3 * width), BF16)]
        + [shape(s, BF16) for s in slots[1:]]
    )
    return pl.pallas_call(
        functools.partial(forward_kernel, lay, seqs, length, cuts),
        out_shape=outs,
        in_specs=[vmem] * 7,
        out_specs=[vmem] * 8 + [anyspace] * 3,
        scratch_shapes=[
            pltpu.VMEM(slots[0], BF16),
            pltpu.VMEM((seqs, length, length), F32),
            pltpu.VMEM((seqs, 4, length, 128), F32),
                pltpu.VMEM((total, 80, 256), BF16),
            pltpu.VMEM((seqs, 8, 256), F32),
                pltpu.SemaphoreType.DMA((flows * lay.hops,)),
            pltpu.SemaphoreType.DMA((flows * lay.hops,)),
            pltpu.SemaphoreType.DMA((2,)),
            pltpu.SemaphoreType.DMA((2,)),
            pltpu.SemaphoreType.DMA((4,)),
        ],
        compiler_params=pltpu.CompilerParams(
            collective_id=0, has_side_effects=True, vmem_limit_bytes=VMEM_LIMIT
        ),
        name="forward_attention",
    )(tokens, ids, bias, *shards)


def normalize(values):
    center = values - jnp.mean(values, axis=-1, keepdims=True)
    scale = lax.rsqrt(jnp.mean(center * center, axis=-1, keepdims=True) + EPSILON)
    return center * scale, scale


def normalize_grad(grad, unit, scale):
    return (
        grad
        - jnp.mean(grad, axis=-1, keepdims=True)
        - unit * jnp.mean(grad * unit, axis=-1, keepdims=True)
    ) * scale


def rows_sum(values):
    return jnp.sum(values, axis=0, keepdims=True)


def dense_kernel(
    lay, row_blocks, chunk, direct,
    tokens, att, den, cot, mix_b, up_b, down_b, gain1, shift1, gain2, shift2, g_mix, g_up, g_down,
    layer_out, pre_out, given_out, tok_t, d_mix, d_up, d_down, sums,
    w_mix, w_up, w_down, mix_raw, act, up_g, hid_t, down_t, att_t, mix_g, slope, acc, sem,
):
    step = pl.program_id(0)
    block, width = tokens.shape
    ff = act.shape[1]
    chunks = ff // chunk
    mix_a, mix_w = d_mix.shape[-2:]
    up_w = d_up.shape[-1]
    down_a, down_w = d_down.shape[-2:]

    def fetch_mix():
        return [pltpu.make_async_copy(g_mix, mix_raw, sem.at[0])]

    def fetch_up():
        if not direct:
            return [pltpu.make_async_copy(g_up, w_up, sem.at[1])]
        return [
            pltpu.make_async_copy(g_up.at[c // 2, c % 2], w_up.at[:, :, :, pl.ds(c * up_w, up_w)], sem.at[3 + c])
            for c in range(lay.C)
        ]

    def fetch_down():
        if not direct:
            return [pltpu.make_async_copy(g_down, w_down, sem.at[2])]
        return [
            pltpu.make_async_copy(
                g_down.at[c // 2, c % 2, r // lay.Y, r % lay.Y],
                w_down.at[c, :, pl.ds(r * down_w, down_w)],
                sem.at[3 + lay.C + c * lay.R + r],
            )
            for c in range(lay.C)
            for r in range(lay.R)
        ]

    def up_chunk(lanes):
        return w_up[:, :, :, lanes].reshape(width, chunk)

    def down_chunk(lanes):
        return w_down[:, :, lanes].reshape(width, chunk)

    @pl.when(step == 0)
    def _():
        for copy in fetch_mix() + fetch_up() + fetch_down():
            copy.start()
        acc[...] = jnp.zeros_like(acc)
        for copy in fetch_mix():
            copy.wait()
        unslot(mix_raw, w_mix, lay, mix_a, mix_w, False)

    @pl.when(step < row_blocks)
    def _():
        rows = pl.ds(pl.multiple_of(step * block, block), block)
        att_low = att[...].astype(BF16)
        att_t[:, rows] = jnp.transpose(att_low)
        tok_t[...] = jnp.transpose(tokens[...])
        mixed = dot(att_low, w_mix[...]) + mix_b[...]
        unit1, scale1 = normalize(tokens[...].astype(F32) + mixed)
        hidden = unit1 * gain1[...] + shift1[...]
        hidden_low = hidden.astype(BF16)
        hid_t[:, rows] = jnp.transpose(hidden_low)

        @pl.when(step == 0)
        def _():
            for copy in fetch_up() + fetch_down():
                copy.wait()

        def up_down(n, total):
            lanes = pl.ds(pl.multiple_of(n * chunk, chunk), chunk)
            up = dot(hidden_low, up_chunk(lanes)) + up_b[:, lanes]
            cdf = 0.5 + 0.5 * lax.erf(up * math.sqrt(0.5))
            density = jnp.exp(up * up * -0.5) * (1.0 / math.sqrt(2.0 * math.pi))
            slope[:, lanes] = cdf + up * density
            active = (up * cdf).astype(BF16)
            act[rows, lanes] = active
            return total + dot(active, down_chunk(lanes), NT)

        down = lax.fori_loop(0, chunks, up_down, jnp.zeros((block, width), F32)) + down_b[...]
        unit2, scale2 = normalize(hidden + down)
        layer_out[...] = (unit2 * gain2[...] + shift2[...]).astype(BF16)
        given = cot[...]
        acc[3:4, 0:width] += rows_sum(given * unit2)
        acc[3:4, width : 2 * width] += rows_sum(given)
        sum_grad = normalize_grad(given * gain2[...], unit2, scale2)
        down_grad = sum_grad.astype(BF16)
        down_t[:, rows] = jnp.transpose(down_grad)
        acc[2:3, 3 * width : 4 * width] += rows_sum(down_grad.astype(F32))

        def back(n, total):
            lanes = pl.ds(pl.multiple_of(n * chunk, chunk), chunk)
            grad = (dot(down_grad, down_chunk(lanes)) * slope[:, lanes]).astype(BF16)
            up_g[rows, lanes] = grad
            acc[0:1, lanes] += rows_sum(grad.astype(F32))
            return total + dot(grad, up_chunk(lanes), NT)

        hidden_grad = lax.fori_loop(0, chunks, back, sum_grad)
        acc[2:3, width : 2 * width] += rows_sum(hidden_grad * unit1)
        acc[2:3, 2 * width : 3 * width] += rows_sum(hidden_grad)
        pre_grad = normalize_grad(hidden_grad * gain1[...], unit1, scale1)
        pre_out[...] = pre_grad
        mixed_grad = pre_grad.astype(BF16)
        mix_g[rows, :] = mixed_grad
        acc[2:3, 0:width] += rows_sum(mixed_grad.astype(F32))
        att_grad = dot(mixed_grad, w_mix[...], NT)
        denom = den[...]
        inverse = 1.0 / jnp.maximum(denom, FLOOR)
        numer = att_grad * inverse
        weighted = att_grad * att[...]
        upper = weighted.astype(BF16)
        lower = (weighted - upper.astype(F32)).astype(BF16)
        square = same_head().astype(BF16)
        factor = inverse * (denom > FLOOR).astype(F32)
        lane = lax.broadcasted_iota(jnp.int32, (1, 128), 1)
        for t in range(width // 128):
            lanes = slice(t * 128, t * 128 + 128)
            summed = dot(upper[:, lanes], square) + dot(lower[:, lanes], square)
            extra = -summed * factor[:, lanes]
            extra = jnp.concatenate([extra[:, 64:128], extra[:, 0:64]], axis=1)
            extra_hi = extra.astype(BF16).astype(F32)
            for head in (0, 1):
                spare = 64 - 64 * head
                both = (
                    numer[:, lanes] * lane_half(head)
                    + extra_hi * (lane == spare).astype(F32)
                    + (extra - extra_hi) * (lane == spare + 1).astype(F32)
                )
                at = t * 256 + head * 128
                given_out[:, at : at + 128] = both.astype(BF16)

    @pl.when(step >= row_blocks)
    def _():
        n = step - row_blocks
        lanes = pl.ds(pl.multiple_of(n * chunk, chunk), chunk)
        up_part = dot(hid_t[...], up_g[:, lanes]).astype(BF16)
        for i in range(chunk // up_w):
            d_up[i // 2, i % 2] = up_part[:, i * up_w : (i + 1) * up_w].reshape(d_up.shape[2:])
        down_part = dot(down_t[...], act[:, lanes]).astype(BF16)
        for c in range(lay.C):
            for y in range(lay.Y):
                d_down[c // 2, c % 2, 0, y] = down_part[
                    c * down_a : (c + 1) * down_a, y * down_w : (y + 1) * down_w
                ]

    @pl.when(step == row_blocks)
    def _():
        mix_part = dot(att_t[...], mix_g[...]).astype(BF16)
        for c in range(lay.C):
            d_mix[c // 2, c % 2] = mix_part[:, c * mix_w : (c + 1) * mix_w].reshape(d_mix.shape[2:])
        sums[...] = acc[...]


def dense(lay, tokens, att, den, cot, vectors, g_mix, g_up, g_down):
    total, width = tokens.shape
    block = 256 if total % 256 == 0 else total
    row_blocks = total // block
    ff = g_up.shape[-1] * lay.C
    chunk = ff // lay.Z
    up_w, down_w = g_up.shape[-1], g_down.shape[-1]
    direct = up_w % 128 == 0 and down_w % 128 == 0
    slots = [g.shape for g in (g_mix, g_up, g_down)]
    if not direct:
        g_up = g_up.transpose(2, 3, 4, 0, 1, 5).reshape(lay.Z, lay.Y, g_up.shape[4], ff)
        g_down = g_down.transpose(0, 1, 4, 2, 3, 5).reshape(lay.C, g_down.shape[4], ff)
    last = row_blocks - 1
    per = chunk // up_w
    by_row = pl.BlockSpec((block, width), lambda i: (jnp.minimum(i, last), 0))
    fixed = lambda shape: pl.BlockSpec(shape, lambda i: (0,) * len(shape), pipeline_mode=pl.Buffered(1))
    anyspace = pl.BlockSpec(memory_space=pl.ANY)
    later = lambda i: jnp.maximum(i - row_blocks, 0)
    if per == 1:
        up_spec = pl.BlockSpec((1, 1) + slots[1][2:], lambda i: (later(i) // 2, later(i) % 2, 0, 0, 0, 0))
    else:
        up_spec = pl.BlockSpec((per // 2, 2) + slots[1][2:], lambda i: (later(i), 0, 0, 0, 0, 0))
    down_spec = pl.BlockSpec(slots[2][:2] + (1,) + slots[2][3:], lambda i: (0, 0, later(i), 0, 0, 0))
    shape = jax.ShapeDtypeStruct
    return pl.pallas_call(
        functools.partial(dense_kernel, lay, row_blocks, chunk, direct),
        grid=(row_blocks + lay.Z,),
        out_shape=[
            shape((total, width), BF16),
            shape((total, width), F32),
            shape((total, 2 * width), BF16),
            shape((width, total), BF16),
            shape(slots[0], BF16),
            shape(slots[1], BF16),
            shape(slots[2], BF16),
            shape((4, ff), F32),
        ],
        in_specs=[by_row] * 4 + [fixed(v.shape) for v in vectors] + [anyspace] * 3,
        out_specs=[
            by_row,
            by_row,
            pl.BlockSpec((block, 2 * width), lambda i: (jnp.minimum(i, last), 0)),
            pl.BlockSpec((width, block), lambda i: (0, jnp.minimum(i, last))),
            fixed(slots[0]),
            up_spec,
            down_spec,
            fixed((4, ff)),
        ],
        scratch_shapes=[
            pltpu.VMEM((width, width), BF16),
            pltpu.VMEM((lay.Z, lay.Y, slots[1][4], ff), BF16),
            pltpu.VMEM((lay.C, slots[2][4], ff), BF16),
            pltpu.VMEM(slots[0], BF16),
            pltpu.VMEM((total, ff), BF16),
            pltpu.VMEM((total, ff), BF16),
            pltpu.VMEM((width, total), BF16),
            pltpu.VMEM((width, total), BF16),
            pltpu.VMEM((width, total), BF16),
            pltpu.VMEM((total, width), BF16),
            pltpu.VMEM((block, ff), F32),
            pltpu.VMEM((4, ff), F32),
            pltpu.SemaphoreType.DMA((3 + lay.C + lay.C * lay.R,)),
        ],
        compiler_params=pltpu.CompilerParams(vmem_limit_bytes=VMEM_LIMIT),
        name="dense",
    )(tokens, att, den, cot, *vectors, g_mix, g_up, g_down)


class Scatter:
    def __init__(self, place, source, mine, came, second, third, fourth, target, r0, n, y_first, send, recv, base, fetch):
        self.p, self.source, self.mine, self.came = place, source, mine, came
        self.second, self.third, self.fourth, self.target = second, third, fourth, target
        self.rows, self.r0, self.n, self.y_first = pl.ds(r0, n), r0, n, y_first
        self.send, self.recv, self.base, self.fetch = send, recv, base, fetch

    def stage(self, number):
        p, rows, lay, mine = self.p, self.rows, self.p.lay, self.mine
        first, copies = self.base, []
        if number == 0:
            copies.append(
                (self.source.at[:, 1 - p.k, :, :, rows], self.came.at[:, :, :, rows], p.at(k=1 - p.k))
            )
        elif number == 3:
            first += 1 + lay.X - 1 + lay.Y - 1
            for d, z in enumerate(p.zs()):
                copies.append((mine.at[p.x, z, p.y, rows], self.fourth.at[d], p.at(z=z)))
        else:
            along_y = (number == 1) == self.y_first
            landing = self.second if number == 1 else self.third
            first += 1
            if number == 2:
                first += (lay.Y - 1) if self.y_first else (lay.X - 1)
            for d, other in enumerate(p.ys() if along_y else p.xs()):
                if along_y:
                    part = mine.at[:, :, other, rows] if number == 1 else mine.at[p.x, :, other, rows]
                    copies.append((part, landing.at[d], p.at(y=other)))
                else:
                    part = mine.at[other, :, :, rows] if number == 1 else mine.at[other, :, p.y, rows]
                    copies.append((part, landing.at[d], p.at(x=other)))
        return [
            remote(src, dst, self.send.at[first + i], self.recv.at[first + i], device)
            for i, (src, dst, device) in enumerate(copies)
        ]

    def own_copy(self):
        return pltpu.make_async_copy(
            self.source.at[:, self.p.k, :, :, self.rows], self.mine.at[:, :, :, self.rows], self.fetch
        )

    def start(self, number):
        for copy in self.stage(number):
            copy.start()

    def begin(self):
        self.start(0)
        if self.fetch is not None:
            self.own_copy().start()

    def advance(self, number):
        p, rows, lay, mine = self.p, self.rows, self.p.lay, self.mine
        if number == 1 and self.fetch is not None:
            self.own_copy().wait()
        for copy in self.stage(number - 1):
            copy.wait_recv()
        if number == 1:

            def add(i, _):
                x, zy = i // (lay.Z * lay.Y), i % (lay.Z * lay.Y)
                z, y = zy // lay.Y, zy % lay.Y
                mine[x, z, y, rows] = (
                    mine[x, z, y, rows].astype(F32) + self.came[x, z, y, rows].astype(F32)
                ).astype(BF16)
                return 0

            lax.fori_loop(0, lay.X * lay.Z * lay.Y, add, 0)
        elif number == 2:
            outer = lay.X if self.y_first else lay.Z
            inner = lay.Z if self.y_first else lay.Y

            def add(i, _):
                a, b = i // inner, i % inner
                total = jnp.zeros((self.n, mine.shape[-1]), F32)
                for d in range(self.second.shape[0]):
                    total = total + self.second[d, a, b].astype(F32)
                if self.y_first:
                    mine[a, b, p.y, rows] = (mine[a, b, p.y, rows].astype(F32) + total).astype(BF16)
                else:
                    mine[p.x, a, b, rows] = (mine[p.x, a, b, rows].astype(F32) + total).astype(BF16)
                return 0

            lax.fori_loop(0, outer * inner, add, 0)
        elif number == 3:

            def add(z, _):
                total = mine[p.x, z, p.y, rows].astype(F32)
                for d in range(self.third.shape[0]):
                    total = total + self.third[d, z].astype(F32)
                mine[p.x, z, p.y, rows] = total.astype(BF16)
                return 0

            lax.fori_loop(0, lay.Z, add, 0)
        else:
            total = mine[p.x, p.z, p.y, rows].astype(F32)
            for d in range(lay.Z - 1):
                total = total + self.fourth[d].astype(F32)
            self.target[rows, :] = total
            return
        self.start(number)

    def sent(self):
        for number in range(4):
            for copy in self.stage(number):
                copy.wait_send()


def backward_kernel(
    lay, seqs, length, cuts, *refs
):
    (carry, ids, prev, tok_t, sums, q_hbm, k_hbm, v_hbm, given_hbm, full_in, pre, d_mix, d_up, d_down) = refs[:14]
    (tokens_grad, o_in, o_mix, o_up, o_down, o_sums) = refs[14:20]
    rest = list(refs[20:])
    (mask, tab, out_state, in_state, flags, key_part, value_part, grads, held, given_in, d_in, vec, vec_in,
     mine_mix, mine_up, mine_down, came_mix, came_up, came_down, came_in) = rest[:20]
    send, recv, misc_send, misc_recv, local = rest[-5:]
    landing = rest[20:-5]
    p = Place(lay)
    _, total_rows, width = held.shape
    q_in, k_in, v_in = held.at[0], held.at[1], held.at[2]
    pairs = width // 128
    total = seqs * pairs
    spot = local.shape[0] - 4
    loads = [
        pltpu.make_async_copy(src, dst, local.at[spot + i])
        for i, (src, dst) in enumerate(((q_hbm, q_in), (k_hbm, k_in), (v_hbm, v_in), (given_hbm, given_in)))
    ]
    for copy in loads:
        copy.start()
    p.barrier()

    groups, base, used = [], 0, 0
    for index, (source, mine, came, target, parts) in enumerate(
        (
            (d_down, mine_down, came_down, o_down, cuts[0]),
            (d_up, mine_up, came_up, o_up, cuts[1]),
            (d_mix, mine_mix, came_mix, o_mix, cuts[2]),
            (d_in, d_in.at[:, p.k], came_in, o_in, cuts[3]),
        )
    ):
        group = []
        for r0, n, y_first in parts:
            second, third, fourth = landing[3 * used : 3 * used + 3]
            fetch = local.at[used] if index < 3 else None
            group.append(
                Scatter(p, source, mine, came, second, third, fourth, target, r0, n, y_first, send, recv, base, fetch)
            )
            base += lay.hops
            used += 1
        groups.append(group)
    for group in groups[:3]:
        for flow in group:
            flow.begin()

    def pre_copy(b):
        return pltpu.make_async_copy(pre.at[pl.ds(b * 256, 256)], key_part.at[pl.ds(b * 256, 256)], misc_recv.at[2 + b])

    def grad_copy(b):
        return pltpu.make_async_copy(value_part.at[pl.ds(b * 256, 256)], tokens_grad.at[pl.ds(b * 256, 256)], misc_send.at[2 + b])

    blocks = total_rows // 256

    cos_a, sin_a, _, _ = angle_tables(length)
    cos_e, sin_e = edge_angles(cos_a, sin_a, length)
    for s in range(seqs):
        _, _, carried, last_mask, passes = seq_masks(ids, prev, s, length, p.c > 0)
        tab[s, 0] = cos_a * carried
        tab[s, 1] = sin_a * carried
        tab[s, 2] = cos_e * last_mask
        tab[s, 3] = sin_e * last_mask
        flags[s] = jnp.broadcast_to(passes, (8, 256))
    for copy in loads:
        copy.wait()

    def where(it):
        s, pair = it // pairs, it % pairs
        return s, pl.ds(pl.multiple_of(s * length, length), length), pl.ds(pl.multiple_of(pair * 128, 128), 128)

    def given_of(it):
        s, pair = it // pairs, it % pairs
        rows = pl.ds(pl.multiple_of(s * length, length), length)
        lane = lax.broadcasted_iota(jnp.int32, (1, 128), 1)
        plus = [given_in[rows, pl.ds(pl.multiple_of(pair * 256 + 128 * head, 128), 128)] for head in (0, 1)]
        given = plus[0] * lane_half(0).astype(BF16) + plus[1] * lane_half(1).astype(BF16)
        extra = jnp.zeros((length, 128), F32)
        for head in (0, 1):
            spare = 64 - 64 * head
            own = ((lane == spare) | (lane == spare + 1)).astype(F32)
            one = jnp.sum(plus[head].astype(F32) * own, axis=1, keepdims=True)
            extra = extra + one * lane_half(head)
        return plus, given, extra

    def local_state(it, _):
        s, rows, lanes = where(it)
        _, given, extra = given_of(it)
        queries, given = q_in[rows, lanes], given.astype(F32)
        scaled = jnp.concatenate([given * tab[s, 0], given * tab[s, 1]], axis=1).astype(BF16)
        state = dot(queries, scaled, TN)
        wide = queries.astype(F32) * extra
        for part in (0, 1):
            packed = pack_state(state[:, part * 128 : part * 128 + 128])
            out_state[it, 0:64, part * 128 : part * 128 + 128] = packed.astype(BF16)
            total_row = jnp.sum(wide * tab[s, part], axis=0, keepdims=True)
            out_state[it, 64:80, part * 128 : part * 128 + 128] = jnp.broadcast_to(total_row, (16, 128)).astype(BF16)
        return 0

    lax.fori_loop(0, total, local_state, 0)

    def chain_copy():
        return remote(out_state, in_state, misc_send.at[1], misc_recv.at[1], p.ring(-1))

    turn_c, turn_s = math.cos(OMEGA * length), math.sin(OMEGA * length)

    def hand_on():
        def one(it, _):
            came = in_state[it].astype(F32)
            came_c, came_s = came[:, 0:128], came[:, 128:256]
            turned = jnp.concatenate(
                [came_c * turn_c - came_s * turn_s, came_c * turn_s + came_s * turn_c], axis=1
            )
            state = out_state[it].astype(F32) + flags[it // pairs, 0:1, :] * turned
            out_state[it] = state.astype(BF16)
            return 0

        lax.fori_loop(0, total, one, 0)

    def chain_step():
        @pl.when(p.c == lay.C - 1)
        def _():
            in_state[...] = jnp.zeros_like(in_state)

        @pl.when(p.c < lay.C - 1)
        def _():
            chain_copy().wait_recv()
            hand_on()

        @pl.when(p.c > 0)
        def _():
            chain_copy().start()

    def line(number, group):
        return [functools.partial(flow.advance, number) for flow in groups[group]]

    order = [(1, 0), (1, 1), (2, 0), (1, 2), (2, 1), (3, 0), (2, 2), (3, 1), (4, 0), (3, 2), (4, 1), (4, 2)]
    thunks = [thunk for number, group in order for thunk in line(number, group)]
    inside = (len(thunks) * 2) // 3
    block = 256 if length % 256 == 0 else length

    def local_attention(it, _):
        @pl.when(it == ((lay.C - 1 - p.c) * total) // lay.C)
        def _():
            chain_step()

        for n, thunk in enumerate(thunks[:inside]):

            @pl.when(it == (n * total) // inside)
            def _(thunk=thunk):
                thunk()

        s, rows, lanes = where(it)
        for seq in range(seqs):

            @pl.when(it == seq * pairs)
            def _(seq=seq):
                row, column, _, _, _ = seq_masks(ids, prev, seq, length, p.c > 0)
                at_j = lax.broadcasted_iota(jnp.int32, (length, length), 0)
                at_i = lax.broadcasted_iota(jnp.int32, (length, length), 1)
                allowed = (column[:, 0:1] == row) & (at_j <= at_i)
                cos_a, sin_a, cos_r, sin_r = angle_tables(length)
                mask[...] = jnp.where(allowed, cos_a[:, 0:1] * cos_r + sin_a[:, 0:1] * sin_r, 0.0)

        lane = lax.broadcasted_iota(jnp.int32, (1, 128), 1)
        queries, keys, values = q_in[rows, lanes], k_in[rows, lanes], v_in[rows, lanes]
        plus, given, extra = given_of(it)
        query_total = jnp.zeros((length, 128), F32)
        for head in (0, 1):
            side = lane_half(head)
            only = side.astype(BF16)
            spare = 64 - 64 * head
            given_plus = plus[head]
            ones = ((lane == spare) | (lane == spare + 1)).astype(BF16)
            value_plus = values * only + ones
            key_only, query_only, given_only = keys * only, queries * only, given * only
            query_parts = []
            for b in range(length // block):
                lo = b * block
                scores = dot(key_only[lo : lo + block], queries[lo:], NT) * mask[lo : lo + block, lo:]
                grads_ji = (
                    dot(value_plus[lo : lo + block], given_plus[lo:], NT) * mask[lo : lo + block, lo:]
                ).astype(BF16)
                here = pl.ds(pl.multiple_of(s * length + lo, block), block)
                key_add = dot(grads_ji, query_only[lo:])
                value_add = dot(scores.astype(BF16), given_only[lo:])
                if head == 0:
                    key_part[here, lanes] = key_add
                    value_part[here, lanes] = value_add
                else:
                    key_part[here, lanes] += key_add
                    value_part[here, lanes] += value_add
                add = dot(grads_ji, key_only[lo : lo + block], TN)
                if lo:
                    query_total = jnp.concatenate([query_total[:lo], query_total[lo:] + add], axis=0)
                else:
                    query_total = query_total + add
        state_c, state_s = unpack_state(carry[it])
        wide = jnp.concatenate([state_c, state_s], axis=0).astype(BF16)
        reach = dot(given, wide, NT)
        totals = carry[it, 64:80, :].astype(F32)[0:1]
        query_total = query_total + tab[s, 0] * (reach[:, 0:128] + extra * totals[:, 0:128])
        query_total = query_total + tab[s, 1] * (reach[:, 128:256] + extra * totals[:, 128:256])
        grads[rows, lanes] = jnp.where(queries.astype(F32) > 0.0, query_total, 0.0).astype(BF16)
        return 0

    lax.fori_loop(0, total, local_attention, 0)

    def finish(it, _):
        s, rows, lanes = where(it)
        pair = it % pairs
        keys, values = k_in[rows, lanes], v_in[rows, lanes]
        state_c, state_s = unpack_state(in_state[it])
        by_row = jnp.concatenate([state_c, state_s], axis=0).astype(BF16)
        by_lane = jnp.concatenate([state_c, state_s], axis=1).astype(BF16)
        totals = in_state[it, 64:80, :].astype(F32)[0:1]
        c_j, s_j = tab[s, 2], tab[s, 3]
        key_reach = dot(values, by_row, NT) + totals
        value_reach = dot(keys, by_lane)
        key_grad = key_part[rows, lanes] + c_j * key_reach[:, 0:128] + s_j * key_reach[:, 128:256]
        value_grad = value_part[rows, lanes] + c_j * value_reach[:, 0:128] + s_j * value_reach[:, 128:256]
        key_lanes = pl.ds(pl.multiple_of(width + pair * 128, 128), 128)
        value_lanes = pl.ds(pl.multiple_of(2 * width + pair * 128, 128), 128)
        grads[rows, key_lanes] = jnp.where(keys.astype(F32) > 0.0, key_grad, 0.0).astype(BF16)
        grads[rows, value_lanes] = value_grad.astype(BF16)
        return 0

    lax.fori_loop(0, total, finish, 0)
    for b in range(blocks):
        pre_copy(b).start()
    thirds = [
        pltpu.make_async_copy(
            full_in.at[:, pl.ds(i * width, width)], held.at[i, pl.ds(0, width)], local.at[spot + i]
        )
        for i in range(3)
    ]
    for copy in thirds:
        copy.start()
    vec[0] = sums[...]

    def bias_sum(n, _):
        lanes = pl.ds(pl.multiple_of(n * 256, 256), 256)
        vec[0, 1:2, lanes] = rows_sum(grads[:, lanes].astype(F32))
        return 0

    lax.fori_loop(0, 3 * width // 256, bias_sum, 0)

    in_a, in_w = o_in.shape
    piece = math.lcm(in_w, 128)
    for n in range(3 * width // piece):
        for m in range(width // 256):
            part = dot(tok_t[m * 256 : (m + 1) * 256, :], grads[:, n * piece : (n + 1) * piece]).astype(BF16)
            for i in range(piece // in_w):
                c = n * (piece // in_w) + i
                lo = m * 256
                while lo < (m + 1) * 256:
                    r = lo // in_a
                    hi = min((r + 1) * in_a, (m + 1) * 256)
                    d_in[c // 2, c % 2, r // lay.Y, r % lay.Y, lo - r * in_a : hi - r * in_a, :] = part[
                        lo - m * 256 : hi - m * 256, i * in_w : (i + 1) * in_w
                    ]
                    lo = hi
    for flow in groups[3]:
        flow.begin()

    def vector_stage(number):
        first = (0, 1, lay.X, lay.X + lay.Y - 1)[number]
        peers = (
            [p.at(k=1 - p.k)],
            [p.at(x=x) for x in p.xs()],
            [p.at(y=y) for y in p.ys()],
            [p.at(z=z) for z in p.zs()],
        )[number]
        shift = 2 + blocks + first
        return [
            remote(vec.at[number], vec_in.at[first + i], misc_send.at[shift + i], misc_recv.at[shift + i], peer)
            for i, peer in enumerate(peers)
        ]

    def vector_start(number):
        for copy in vector_stage(number):
            copy.start()

    def vector_add(number):
        total_vec = vec[number]
        first = (0, 1, lay.X, lay.X + lay.Y - 1)[number]
        for i, copy in enumerate(vector_stage(number)):
            copy.wait_recv()
            total_vec = total_vec + vec_in[first + i]
        if number == 3:
            o_sums[...] = total_vec
        else:
            vec[number + 1] = total_vec
            vector_start(number + 1)

    vector_start(0)
    for thunk in thunks[inside:]:
        thunk()
    tail = []
    for number in (1, 2, 3, 4):
        tail += line(number, 3)
        tail.append(functools.partial(vector_add, number - 1))
    done = 0
    for copy in thirds:
        copy.wait()
    for b in range(blocks):
        pre_copy(b).wait()
        part = slice(b * 256, (b + 1) * 256)
        out = key_part[part, :]
        for i in range(3):
            out = out + dot(grads[part, i * width : (i + 1) * width], held[i, 0:width, :], NT)
        value_part[part, :] = out
        grad_copy(b).start()
        upto = (len(tail) * (b + 1)) // (blocks + 1)
        for thunk in tail[done:upto]:
            thunk()
        done = upto
    for thunk in tail[done:]:
        thunk()
    for b in range(blocks):
        grad_copy(b).wait()
    for group in groups:
        for flow in group:
            flow.sent()
    for number in range(4):
        for copy in vector_stage(number):
            copy.wait_send()

    @pl.when(p.c > 0)
    def _():
        chain_copy().wait_send()


def backward(lay, ids, prev, q, k, v, given, carry, tok_t, full_in, sums, pre, d_mix, d_up, d_down, in_shape):
    seqs, length = ids.shape
    rows, width = q.shape
    total = seqs * (width // 128)
    in_slots = (lay.X, 2, lay.Z, lay.Y) + in_shape
    sources = (d_down, d_up, d_mix, in_slots)
    slots = [s if isinstance(s, tuple) else s.shape for s in sources]
    cuts = tuple(pieces(s[4], 1) for s in slots)
    landing = []
    for slot, parts in zip(slots, cuts, strict=True):
        for _, n, y_first in parts:
            tile = (n, slot[5])
            if y_first:
                landing += [(lay.Y - 1, lay.X, lay.Z) + tile, (lay.X - 1, lay.Z) + tile]
            else:
                landing += [(lay.X - 1, lay.Z, lay.Y) + tile, (lay.Y - 1, lay.Z) + tile]
            landing.append((lay.Z - 1,) + tile)
    flows = sum(len(c) for c in cuts)
    vmem, anyspace = pl.BlockSpec(memory_space=pltpu.VMEM), pl.BlockSpec(memory_space=pl.ANY)
    shape = jax.ShapeDtypeStruct
    ff = sums.shape[1]
    blocks = rows // 256
    half = [(s[0],) + s[2:] for s in slots]
    hop = lay.hops
    misc = 2 + blocks + hop
    scratch = [
        pltpu.VMEM((length, length), F32),
        pltpu.VMEM((seqs, 4, length, 128), F32),
        pltpu.VMEM((total, 80, 256), BF16),
        pltpu.VMEM((total, 80, 256), BF16),
        pltpu.VMEM((seqs, 8, 256), F32),
        pltpu.VMEM((rows, width), F32),
        pltpu.VMEM((rows, width), F32),
        pltpu.VMEM((rows, 3 * width), BF16),
        pltpu.VMEM((3, rows, width), BF16),
        pltpu.VMEM((rows, 2 * width), BF16),
        pltpu.VMEM(in_slots, BF16),
        pltpu.VMEM((4, 4, ff), F32),
        pltpu.VMEM((hop, 4, ff), F32),
    ]
    scratch += [pltpu.VMEM(half[i], BF16) for i in (2, 1, 0)] + [pltpu.VMEM(half[i], BF16) for i in (2, 1, 0, 3)]
    scratch += [pltpu.VMEM(s, BF16) for s in landing]
    scratch += [
        pltpu.SemaphoreType.DMA((flows * hop,)),
        pltpu.SemaphoreType.DMA((flows * hop,)),
        pltpu.SemaphoreType.DMA((misc,)),
        pltpu.SemaphoreType.DMA((misc,)),
        pltpu.SemaphoreType.DMA((flows + 4,)),
    ]
    return pl.pallas_call(
        functools.partial(backward_kernel, lay, seqs, length, cuts),
        out_shape=[shape((rows, width), F32)]
        + [shape(slots[i][4:], F32) for i in (3, 2, 1, 0)]
        + [shape((4, ff), F32)],
        in_specs=[vmem] * 5 + [anyspace] * 9,
        out_specs=[anyspace] + [vmem] * 5,
        scratch_shapes=scratch,
        compiler_params=pltpu.CompilerParams(
            collective_id=1, has_side_effects=True, vmem_limit_bytes=VMEM_LIMIT
        ),
        name="backward_attention",
    )(carry, ids, prev, tok_t, sums, q, k, v, given, full_in, pre, d_mix, d_up, d_down)


def per_device(
    tokens, segment_ids, in_weight, in_bias, mix_weight, mix_bias, first_gain, first_shift,
    up_weight, up_bias, down_weight, down_bias, second_gain, second_shift, cotangent,
):
    lay = Layout(lax.axis_size("row"), lax.axis_size("col"))
    seqs, length, width = tokens.shape
    flat = tokens.reshape(seqs * length, width)
    line = lambda v: v.astype(F32)[None]
    q, k, v, att, den, carry, prev, full_in, g_mix, g_up, g_down = forward(
        lay, flat, segment_ids, line(in_bias), (in_weight, mix_weight, up_weight, down_weight.T)
    )
    vectors = [line(u) for u in (mix_bias, up_bias, down_bias, first_gain, first_shift, second_gain, second_shift)]
    layer_out, pre, given, tok_t, d_mix, d_up, d_down, sums = dense(
        lay, flat, att, den, cotangent.reshape(seqs * length, width), vectors, g_mix, g_up, g_down
    )
    tokens_grad, o_in, o_mix, o_up, o_down, o_sums = backward(
        lay, segment_ids, prev, q, k, v, given, carry, tok_t, full_in, sums, pre, d_mix, d_up, d_down,
        in_weight.shape,
    )
    part = lambda row, n: o_sums[row, n * width : (n + 1) * width]
    return (
        layer_out.reshape(tokens.shape),
        tokens_grad.reshape(tokens.shape),
        o_in,
        o_sums[1, : 3 * width],
        o_mix,
        part(2, 0),
        part(2, 1),
        part(2, 2),
        o_up,
        o_sums[0],
        o_down.T,
        part(2, 3),
        part(3, 0),
        part(3, 1),
    )


def solution(mesh):
    block, matrix, rep = P("row", "col", None), P("row", "col"), P()
    return jax.shard_map(
        per_device,
        mesh=mesh,
        in_specs=(block, matrix, matrix, rep, matrix, rep, rep, rep, matrix, rep, matrix, rep, rep, rep, block),
        out_specs=(block, block, matrix, rep, matrix, rep, rep, rep, matrix, rep, matrix, rep, rep, rep),
        check_vma=False,
    )
```

```python
import functools
import math

import jax
import jax.numpy as jnp
from jax import lax
from jax.experimental import pallas as pl
from jax.experimental.pallas import tpu as pltpu
from jax.sharding import PartitionSpec as P

HEADS = 12
HEAD_DIM = 64
DOC_MAX = 2000
EPSILON = 1e-05
FLOOR = 4.0
OMEGA = math.pi / (2.0 * DOC_MAX)
MESH = pl.DeviceIdType.MESH
F32 = jnp.float32
BF16 = jnp.bfloat16
VMEM_LIMIT = 67_043_328

NN = (((1,), (0,)), ((), ()))
NT = (((1,), (1,)), ((), ()))
TN = (((0,), (0,)), ((), ()))


def dot(first, second, dims=NN):
    return lax.dot_general(first, second, dims, preferred_element_type=F32)


class Layout:
    def __init__(self, rows, cols):
        self.R, self.C = rows, cols
        self.Z = 4 if rows % 4 == 0 else rows
        self.Y = rows // self.Z
        self.K = 2
        self.X = cols // 2
        self.hops = (self.Z - 1) + (self.Y - 1) + (self.X - 1) + 1


class Place:
    def __init__(self, lay):
        self.lay = lay
        self.r = lax.axis_index("row")
        self.c = lax.axis_index("col")
        self.z, self.y = self.r // lay.Y, self.r % lay.Y
        self.x, self.k = self.c // 2, self.c % 2

    def at(self, z=None, y=None, x=None, k=None):
        z = self.z if z is None else z
        y = self.y if y is None else y
        x = self.x if x is None else x
        k = self.k if k is None else k
        return {"row": z * self.lay.Y + y, "col": x * 2 + k}

    def zs(self):
        return [lax.rem(self.z + d, self.lay.Z) for d in range(1, self.lay.Z)]

    def ys(self):
        return [lax.rem(self.y + d, self.lay.Y) for d in range(1, self.lay.Y)]

    def xs(self):
        return [lax.rem(self.x + d, self.lay.X) for d in range(1, self.lay.X)]

    def ring(self, step):
        return {"row": self.r, "col": lax.rem(self.c + step + self.lay.C, self.lay.C)}

    def barrier(self):
        peers = [self.at(z=z) for z in self.zs()] + [self.at(y=y) for y in self.ys()]
        peers += [self.at(x=x) for x in self.xs()] + [self.at(k=1 - self.k)]
        peers += [self.ring(1), self.ring(-1)]
        sem = pltpu.get_barrier_semaphore()
        for peer in peers:
            pl.semaphore_signal(sem, inc=1, device_id=peer, device_id_type=MESH)
        pl.semaphore_wait(sem, len(peers))


def remote(src, dst, send, recv, device):
    return pltpu.make_async_remote_copy(
        src_ref=src, dst_ref=dst, send_sem=send, recv_sem=recv, device_id=device, device_id_type=MESH
    )


class Gather:
    def __init__(self, place, shard, whole, r0, n, y_first, send, recv, base):
        self.p, self.shard, self.whole = place, shard, whole
        self.rows = pl.ds(r0, n)
        self.y_first = y_first
        self.send, self.recv, self.base = send, recv, base

    def stage(self, number):
        p, g, rows, lay = self.p, self.whole, self.rows, self.p.lay
        first, copies = self.base, []
        if number == 0:
            for z in p.zs():
                copies.append((self.shard.at[rows], g.at[p.x, p.k, p.z, p.y, rows], p.at(z=z)))
        else:
            first += lay.Z - 1
            along_y = (number == 1) == self.y_first
            if number == 3:
                part = g.at[:, p.k, :, :, rows]
                copies.append((part, part, p.at(k=1 - p.k)))
                first += lay.Y - 1 + lay.X - 1
            else:
                if number == 2:
                    first += (lay.Y - 1) if self.y_first else (lay.X - 1)
                    part = g.at[:, p.k, :, p.y, rows] if along_y else g.at[p.x, p.k, :, :, rows]
                else:
                    part = g.at[p.x, p.k, :, p.y, rows]
                for peer in [p.at(y=y) for y in p.ys()] if along_y else [p.at(x=x) for x in p.xs()]:
                    copies.append((part, part, peer))
        return [
            remote(src, dst, self.send.at[first + i], self.recv.at[first + i], device)
            for i, (src, dst, device) in enumerate(copies)
        ]

    def start(self, number):
        for copy in self.stage(number):
            copy.start()

    def arrive(self, number):
        for copy in self.stage(number):
            copy.wait_recv()

    def advance(self, number):
        self.arrive(number - 1)
        self.start(number)

    def sent(self, numbers):
        for number in numbers:
            for copy in self.stage(number):
                copy.wait_send()


def pieces(rows, count):
    tiles, many = rows // 16, 2 * count
    many = min(many, tiles)
    cuts = [(tiles * i + many - 1) // many for i in range(many + 1)]
    return [(cuts[i] * 16, (cuts[i + 1] - cuts[i]) * 16, i % 2 == 1) for i in range(many)]


def lane_half(head):
    lane = lax.broadcasted_iota(jnp.int32, (1, 128), 1)
    return ((lane < 64) if head == 0 else (lane >= 64)).astype(F32)


def same_head():
    row = lax.broadcasted_iota(jnp.int32, (128, 128), 0)
    lane = lax.broadcasted_iota(jnp.int32, (128, 128), 1)
    return ((row < 64) == (lane < 64)).astype(F32)


def seq_masks(ids_ref, prev_ref, seq, length, has_prev):
    row = ids_ref[seq : seq + 1, :].astype(F32)
    column = jnp.transpose(jnp.broadcast_to(row, (128, length)))
    lane = lax.broadcasted_iota(jnp.int32, (1, length), 1)
    first = jnp.sum(jnp.where(lane == 0, row, 0.0), axis=1, keepdims=True)
    last = jnp.sum(jnp.where(lane == length - 1, row, 0.0), axis=1, keepdims=True)
    before = prev_ref[seq : seq + 1, :].astype(F32)
    before = jnp.sum(jnp.where(lane == length - 1, before, 0.0), axis=1, keepdims=True)
    before = jnp.where(has_prev, before, -1.0)
    carry = (column == before).astype(F32)
    last_mask = (column == last).astype(F32)
    passes = ((first == last) & (first == before)).astype(F32)
    return row, column, carry, last_mask, passes


def angle_tables(length):
    row = lax.broadcasted_iota(jnp.int32, (1, length), 1).astype(F32) * OMEGA
    rows = jnp.cos(row), jnp.sin(row)
    return *(jnp.transpose(jnp.broadcast_to(r, (128, length))) for r in rows), *rows


def edge_angles(cosine, sine, length):
    turn_c, turn_s = math.cos(OMEGA * length), math.sin(OMEGA * length)
    return cosine * turn_c + sine * turn_s, sine * turn_c - cosine * turn_s


def unpack_state(block):
    low, high = lane_half(0), lane_half(1)
    out = []
    for half in (0, 1):
        part = block[0:64, half * 128 : half * 128 + 128].astype(F32)
        out.append(jnp.concatenate([part * low, part * high], axis=0))
    return out


def pack_state(square):
    square = square * same_head()
    return square[0:64] + square[64:128]


def unslot(whole, flat, lay, a, b, transposed):
    for c in range(lay.C):
        if transposed:
            for r in range(lay.R):
                flat[c * a : (c + 1) * a, r * b : (r + 1) * b] = whole[
                    c // 2, c % 2, r // lay.Y, r % lay.Y
                ]
        else:
            for z in range(lay.Z):
                for y in range(lay.Y):
                    r = z * lay.Y + y
                    flat[r * a : (r + 1) * a, c * b : (c + 1) * b] = whole[c // 2, c % 2, z, y]


def forward_kernel(
    lay, seqs, length, cuts, split,
    tokens, ids, bias_in, in_s, mix_s, up_s, down_s,
    att, den, carry, prev, q_hbm, k_hbm, v_hbm, in_hbm, mix_hbm, tok_hbm, g_up, g_down,
    q_out, k_out, v_out, full_in, full_mix, tok_t, g_in, g_mix, bias, mask, tab, out_state, flags,
    send, recv, misc_send, misc_recv, local,
):
    p = Place(lay)
    pairs = q_out.shape[1] // 128
    width = q_out.shape[1]
    total = seqs * pairs
    outputs = [
        pltpu.make_async_copy(src, dst, local.at[4 + i])
        for i, (src, dst) in enumerate(
            ((q_out, q_hbm), (k_out, k_hbm), (v_out, v_hbm), (full_in, in_hbm), (tok_t, tok_hbm), (full_mix, mix_hbm))
        )
    ]
    p.barrier()
    flows = []
    base = 0
    groups = []
    for shard, whole, parts in zip(
        (in_s, mix_s, up_s, down_s), (g_in, g_mix, g_up, g_down), cuts, strict=True
    ):
        group = []
        for r0, n, y_first in parts:
            group.append(Gather(p, shard, whole, r0, n, y_first, send, recv, base))
            base += lay.hops
        groups.append(group)
        flows += group
    own = [
        pltpu.make_async_copy(shard, whole.at[p.x, p.k, p.z, p.y], local.at[i])
        for i, (shard, whole) in enumerate(
            zip((in_s, mix_s, up_s, down_s), (g_in, g_mix, g_up, g_down), strict=True)
        )
    ]
    for copy in own:
        copy.start()
    ring_ids = remote(ids, prev, misc_send.at[0], misc_recv.at[0], p.ring(1))
    ring_ids.start()
    for flow in flows:
        flow.start(0)
    for copy in own:
        copy.wait()
    for flow in groups[0]:
        flow.advance(1)
    tok_t[...] = jnp.transpose(tokens[...])
    bias[...] = bias_in[...].astype(F32).reshape(bias.shape)
    outputs[4].start()

    cos_a, sin_a, cos_r, sin_r = angle_tables(length)
    cos_e, sin_e = edge_angles(cos_a, sin_a, length)
    ring_ids.wait_recv()
    for s in range(seqs):
        row, column, carried, last_mask, passes = seq_masks(ids, prev, s, length, p.c > 0)
        at_i = lax.broadcasted_iota(jnp.int32, (length, length), 0)
        at_j = lax.broadcasted_iota(jnp.int32, (length, length), 1)
        allowed = (column[:, 0:1] == row) & (at_j <= at_i)
        mask[s] = jnp.where(allowed, cos_a[:, 0:1] * cos_r + sin_a[:, 0:1] * sin_r, 0.0)
        tab[s, 0] = cos_a * carried
        tab[s, 1] = sin_a * carried
        tab[s, 2] = cos_e * last_mask
        tab[s, 3] = sin_e * last_mask
        flags[s] = jnp.broadcast_to(passes, (8, 256))

    for number in (2, 3):
        for flow in groups[0]:
            flow.advance(number)
    for flow in groups[0]:
        flow.arrive(3)

    def onward(number, group):
        for flow in groups[group]:
            flow.advance(number)

    onward(1, 1)
    unslot(g_in, full_in, lay, in_s.shape[0], in_s.shape[1], False)
    outputs[3].start()

    blocks = width // 256
    half = tokens.shape[0] // 2

    def project(target, start, relu):
        def column_block(j, _):
            lanes = pl.ds(pl.multiple_of(j * 256, 256), 256)
            source = pl.ds(pl.multiple_of(start + j * 256, 256), 256)
            for m in range(2):
                out = dot(tokens[m * half : (m + 1) * half, :], full_in[:, source]) + bias[:, source]
                if relu:
                    out = jnp.maximum(out, 0.0)
                target[m * half : (m + 1) * half, lanes] = out.astype(BF16)
            return 0

        lax.fori_loop(0, blocks, column_block, 0)

    project(k_out, width, True)
    onward(1, 2)
    project(v_out, 2 * width, False)
    during = [(2, 1), (2, 2), (3, 1)] if split else [(2, 1), (2, 2), (1, 3), (3, 1)]

    def where(it):
        s, pair = it // pairs, it % pairs
        return s, pl.ds(pl.multiple_of(s * length, length), length), pl.ds(pl.multiple_of(pair * 128, 128), 128)

    def local_state(it, _):
        s, rows, lanes = where(it)
        keys, values = k_out[rows, lanes], v_out[rows, lanes].astype(F32)
        scaled = jnp.concatenate([values * tab[s, 2], values * tab[s, 3]], axis=1).astype(BF16)
        state = dot(keys, scaled, TN)
        wide = keys.astype(F32)
        for part in (0, 1):
            packed = pack_state(state[:, part * 128 : part * 128 + 128])
            out_state[it, 0:64, part * 128 : part * 128 + 128] = packed.astype(BF16)
            total_row = jnp.sum(wide * tab[s, 2 + part], axis=0, keepdims=True)
            out_state[it, 64:80, part * 128 : part * 128 + 128] = jnp.broadcast_to(total_row, (16, 128)).astype(BF16)
        return 0

    lax.fori_loop(0, total, local_state, 0)

    def chain_copy():
        return remote(out_state, carry, misc_send.at[1], misc_recv.at[1], p.ring(1))

    turn_c, turn_s = math.cos(OMEGA * length), math.sin(OMEGA * length)

    def hand_on():
        def one(it, _):
            came = carry[it].astype(F32)
            came_c, came_s = came[:, 0:128], came[:, 128:256]
            turned = jnp.concatenate(
                [came_c * turn_c + came_s * turn_s, came_s * turn_c - came_c * turn_s], axis=1
            )
            state = out_state[it].astype(F32) + flags[it // pairs, 0:1, :] * turned
            out_state[it] = state.astype(BF16)
            return 0

        lax.fori_loop(0, total, one, 0)

    def chain_step():
        @pl.when(p.c == 0)
        def _():
            carry[...] = jnp.zeros_like(carry)

        @pl.when(p.c > 0)
        def _():
            chain_copy().wait_recv()
            hand_on()

        @pl.when(p.c < lay.C - 1)
        def _():
            chain_copy().start()

    pl.when(p.c == 0)(chain_step)
    project(q_out, 0, True)
    for copy in outputs[:3]:
        copy.start()
    pl.when(p.c == 1)(chain_step)
    step_block = 256 if length % 256 == 0 else length
    chain_turn = (total * 2) // 3 + ((p.c - 2) * (total // 3)) // max(lay.C - 2, 1)

    def local_attention(it, _):
        @pl.when((it == chain_turn) & (p.c > 1))
        def _():
            chain_step()

        for n, (number, group) in enumerate(during):

            @pl.when(it == (n * total) // len(during))
            def _(number=number, group=group):
                onward(number, group)

        s, rows, lanes = where(it)
        low, high = lane_half(0), lane_half(1)
        queries, keys, values = q_out[rows, lanes], k_out[rows, lanes], v_out[rows, lanes]
        for b in range(length // step_block):
            lo, reach = b * step_block, (b + 1) * step_block
            q = queries[lo:reach]
            numer = jnp.zeros((step_block, 128), F32)
            denom = jnp.zeros((step_block, 128), F32)
            for side in (low, high):
                only = side.astype(BF16)
                scores = dot(q, keys[:reach] * only, NT) * mask[s, lo:reach, 0:reach]
                numer = numer + dot(scores.astype(BF16), values[:reach] * only)
                denom = denom + jnp.sum(scores, axis=1, keepdims=True) * side
            here = pl.ds(pl.multiple_of(s * length + lo, step_block), step_block)
            att[here, lanes] = numer
            den[here, lanes] = denom
        return 0

    lax.fori_loop(0, total, local_attention, 0)

    square = same_head()

    def finish(it, _):
        s, rows, lanes = where(it)
        state_c, state_s = unpack_state(carry[it])
        totals = []
        for part in (0, 1):
            line = carry[it, 64:80, part * 128 : part * 128 + 128].astype(F32)[0:1]
            totals.append(jnp.transpose(jnp.broadcast_to(line, (128, 128))) * square)
        wide = jnp.concatenate([state_c, state_s, totals[0], totals[1]], axis=1).astype(BF16)
        reach = dot(q_out[rows, lanes], wide)
        c_i, s_i = tab[s, 0], tab[s, 1]
        numer = att[rows, lanes] + c_i * reach[:, 0:128] + s_i * reach[:, 128:256]
        denom = den[rows, lanes] + c_i * reach[:, 256:384] + s_i * reach[:, 384:512]
        den[rows, lanes] = denom
        att[rows, lanes] = numer / jnp.maximum(denom, FLOOR)
        return 0

    lax.fori_loop(0, total, finish, 0)
    for number, group in [(3, 2)] if split else [(3, 2), (2, 3), (3, 3)]:
        onward(number, group)
    for flow in groups[1]:
        flow.arrive(3)
    unslot(g_mix, full_mix, lay, mix_s.shape[0], mix_s.shape[1], False)
    outputs[5].start()
    for flow in groups[2]:
        flow.arrive(3)
    for flow in groups[3]:
        flow.arrive(0 if split else 3)
    for flow in flows:
        flow.sent(range(1) if split and flow in groups[3] else range(4))
    ring_ids.wait_send()
    for copy in outputs:
        copy.wait()

    @pl.when(p.c < lay.C - 1)
    def _():
        chain_copy().wait_send()


def forward(lay, tokens, ids, bias, shards, split):
    seqs, length = ids.shape
    rows, width = tokens.shape
    total = seqs * (width // 128)
    cuts = [pieces(s.shape[0], n) for s, n in zip(shards, (3, 1, 1, 1), strict=True)]
    cuts = tuple(cuts)
    flows = sum(len(c) for c in cuts)
    vmem, anyspace = pl.BlockSpec(memory_space=pltpu.VMEM), pl.BlockSpec(memory_space=pl.ANY)
    slots = [(lay.X, 2, lay.Z, lay.Y) + s.shape for s in shards]
    shape = jax.ShapeDtypeStruct
    copied = [(rows, width)] * 3 + [(width, 3 * width), (width, width), (width, rows)]
    outs = (
        [shape((rows, width), F32)] * 2
        + [shape((total, 80, 256), BF16), shape(ids.shape, jnp.int32)]
        + [shape(s, BF16) for s in copied + slots[2:]]
    )
    return pl.pallas_call(
        functools.partial(forward_kernel, lay, seqs, length, cuts, split),
        out_shape=outs,
        in_specs=[vmem] * 7,
        out_specs=[vmem] * 4 + [anyspace] * 8,
        scratch_shapes=[pltpu.VMEM(s, BF16) for s in copied]
        + [
            pltpu.VMEM(slots[0], BF16),
            pltpu.VMEM(slots[1], BF16),
            pltpu.VMEM((1, 3 * width), F32),
            pltpu.VMEM((seqs, length, length), F32),
            pltpu.VMEM((seqs, 4, length, 128), F32),
                pltpu.VMEM((total, 80, 256), BF16),
            pltpu.VMEM((seqs, 8, 256), F32),
                pltpu.SemaphoreType.DMA((flows * lay.hops,)),
            pltpu.SemaphoreType.DMA((flows * lay.hops,)),
            pltpu.SemaphoreType.DMA((2,)),
            pltpu.SemaphoreType.DMA((2,)),
            pltpu.SemaphoreType.DMA((10,)),
        ],
        compiler_params=pltpu.CompilerParams(
            collective_id=0, has_side_effects=True, vmem_limit_bytes=VMEM_LIMIT
        ),
        name="forward_attention",
    )(tokens, ids, bias, *shards)


def normalize(values):
    center = values - jnp.mean(values, axis=-1, keepdims=True)
    scale = lax.rsqrt(jnp.mean(center * center, axis=-1, keepdims=True) + EPSILON)
    return center * scale, scale


def normalize_grad(grad, unit, scale):
    return (
        grad
        - jnp.mean(grad, axis=-1, keepdims=True)
        - unit * jnp.mean(grad * unit, axis=-1, keepdims=True)
    ) * scale


def rows_sum(values):
    return jnp.sum(values, axis=0, keepdims=True)


def dense_kernel(
    lay, row_blocks, chunk, split, cuts, *refs
):
    tokens, att, den, cot = refs[:4]
    given_vectors = refs[4:11]
    w_mix_in, g_up, g_down = refs[11:14]
    layer_out, pre_out, given_out, d_mix, d_up, d_down_out, sums = refs[14:21]
    rest = refs[21:]
    if split:
        g_down, rest = rest[0], rest[1:]
    (w_mix, w_up, w_down, act, up_g, hid_t, down_t, att_t, mix_g, unit_v, scale_v, grad_v, vectors, acc, sem) = rest[:15]
    step = pl.program_id(0)
    block, width = tokens.shape
    ff = act.shape[1]
    chunks = ff // chunk
    mix_w, up_w = d_mix.shape[-1], d_up.shape[-1]
    down_a, down_w = g_down.shape[-2:] if split else d_down_out.shape[-2:]
    mix_b, down_b, gain1, shift1, gain2, shift2 = [vectors.at[i : i + 1, 0:width] for i in range(1, 7)]
    starts = [0, row_blocks, 2 * row_blocks, 2 * row_blocks + lay.Z, 3 * row_blocks + lay.Z]
    last_step = 3 * row_blocks + 2 * lay.Z - 1

    def fetch_mix():
        return [pltpu.make_async_copy(w_mix_in, w_mix, sem.at[0])]

    def fetch_up():
        if not split:
            return [pltpu.make_async_copy(g_up, w_up, sem.at[1])]
        return [
            pltpu.make_async_copy(g_up.at[c // 2, c % 2], w_up.at[:, :, :, pl.ds(c * up_w, up_w)], sem.at[3 + c])
            for c in range(lay.C)
        ]

    def fetch_down():
        if not split:
            return [pltpu.make_async_copy(g_down, w_down, sem.at[2])]
        return [
            pltpu.make_async_copy(
                g_down.at[c // 2, c % 2, r // lay.Y, r % lay.Y],
                w_down.at[c, :, pl.ds(r * down_w, down_w)],
                sem.at[3 + lay.C + c * lay.R + r],
            )
            for c in range(lay.C)
            for r in range(lay.R)
        ]

    if split:
        d_down, came, landing = rest[15], rest[16], rest[17:-4]
        send, recv, send2, recv2 = rest[-4:]
        p = Place(lay)
        gathers, scatters = [], []
        for n, (r0, size, y_first) in enumerate(cuts):
            gathers.append(Gather(p, None, g_down, r0, size, y_first, send, recv, n * lay.hops))
            scatters.append(
                Scatter(
                    p, d_down, d_down.at[:, p.k], came, landing[n], None, None, None,
                    r0, size, y_first, send2, recv2, n * lay.hops, None,
                )
            )
        out_copy = pltpu.make_async_copy(d_down.at[:, p.k], d_down_out, sem.at[1])

    def up_chunk(lanes):
        return w_up[:, :, :, lanes].reshape(width, chunk)

    def down_chunk(lanes):
        return w_down[:, :, lanes].reshape(width, chunk)

    @pl.when(step == 0)
    def _():
        for copy in fetch_mix() + fetch_up() + ([] if split else fetch_down()):
            copy.start()
        if split:
            p.barrier()
            for flow in gathers:
                flow.start(1)
        for i, vector in enumerate(given_vectors):
            vectors[i : i + 1, 0 : vector.shape[0]] = vector[...].astype(F32).reshape(1, vector.shape[0])
        acc[...] = jnp.zeros_like(acc)
        for copy in fetch_mix():
            copy.wait()

    @pl.when(step < starts[1])
    def _():
        rows = pl.ds(pl.multiple_of(step * block, block), block)
        att_low = att[...].astype(BF16)
        att_t[:, rows] = jnp.transpose(att_low)
        mixed = dot(att_low, w_mix[...]) + mix_b[...]
        unit1, scale1 = normalize(tokens[...].astype(F32) + mixed)
        unit_v[rows, :] = unit1
        scale_v[rows, :] = jnp.broadcast_to(scale1, (block, 128))
        hidden_low = (unit1 * gain1[...] + shift1[...]).astype(BF16)
        hid_t[:, rows] = jnp.transpose(hidden_low)

        @pl.when(step == 0)
        def _():
            for copy in fetch_up():
                copy.wait()

        def up_part(n, _):
            lanes = pl.ds(pl.multiple_of(n * chunk, chunk), chunk)
            up = dot(hidden_low, up_chunk(lanes)) + vectors[0:1, lanes]
            cdf = 0.5 + 0.5 * lax.erf(up * math.sqrt(0.5))
            density = jnp.exp(up * up * -0.5) * (1.0 / math.sqrt(2.0 * math.pi))
            up_g[rows, lanes] = (cdf + up * density).astype(BF16)
            act[rows, lanes] = (up * cdf).astype(BF16)
            if split:

                @pl.when((step == 1) & (n == 1))
                def _():
                    for flow in gathers:
                        flow.advance(2)

                @pl.when((step == starts[1] - 1) & (n == 1))
                def _():
                    for flow in gathers:
                        flow.advance(3)

            return 0

        lax.fori_loop(0, chunks, up_part, 0)

    if split:

        @pl.when(step == starts[1] - 1)
        def _():
            for flow in gathers:
                flow.arrive(3)
            for copy in fetch_down():
                copy.start()

    @pl.when(step == starts[1])
    def _():
        for copy in fetch_down():
            copy.wait()

    @pl.when((step >= starts[1]) & (step < starts[2]))
    def _():
        rows = pl.ds(pl.multiple_of((step - starts[1]) * block, block), block)

        def down_part(n, total):
            lanes = pl.ds(pl.multiple_of(n * chunk, chunk), chunk)
            return total + dot(act[rows, lanes], down_chunk(lanes), NT)

        down = lax.fori_loop(0, chunks, down_part, jnp.zeros((block, width), F32)) + down_b[...]
        hidden = unit_v[rows, :] * gain1[...] + shift1[...]
        unit2, scale2 = normalize(hidden + down)
        layer_out[...] = (unit2 * gain2[...] + shift2[...]).astype(BF16)
        given = cot[...]
        acc[3:4, 0:width] += rows_sum(given * unit2)
        acc[3:4, width : 2 * width] += rows_sum(given)
        sum_grad = normalize_grad(given * gain2[...], unit2, scale2)
        grad_v[rows, :] = sum_grad
        down_grad = sum_grad.astype(BF16)
        down_t[:, rows] = jnp.transpose(down_grad)
        acc[2:3, 3 * width : 4 * width] += rows_sum(down_grad.astype(F32))

    @pl.when((step >= starts[2]) & (step < starts[3]))
    def _():
        n = step - starts[2]
        lanes = pl.ds(pl.multiple_of(n * chunk, chunk), chunk)
        part = dot(down_t[...], act[:, lanes]).astype(BF16)
        for c in range(lay.C):
            for y in range(lay.Y):
                tile = part[c * down_a : (c + 1) * down_a, y * down_w : (y + 1) * down_w]
                if split:
                    d_down[c // 2, c % 2, n, y] = tile
                else:
                    d_down_out[c // 2, c % 2, 0, y] = tile

    if split:

        @pl.when(step == starts[3])
        def _():
            for flow in scatters:
                flow.start(0)

        @pl.when(step == starts[3] + 1)
        def _():
            for flow in scatters:
                flow.advance(1)

        @pl.when(step == last_step)
        def _():
            for flow in scatters:
                flow.add(2)
            out_copy.start()
            for flow in gathers:
                flow.sent(range(1, 4))
            for flow in scatters:
                flow.sent(range(2))
            out_copy.wait()

    @pl.when((step >= starts[3]) & (step < starts[4]))
    def _():
        rows = pl.ds(pl.multiple_of((step - starts[3]) * block, block), block)
        sum_grad = grad_v[rows, :]
        down_grad = sum_grad.astype(BF16)

        def back(n, total):
            lanes = pl.ds(pl.multiple_of(n * chunk, chunk), chunk)
            grad = (dot(down_grad, down_chunk(lanes)) * up_g[rows, lanes].astype(F32)).astype(BF16)
            up_g[rows, lanes] = grad
            acc[0:1, lanes] += rows_sum(grad.astype(F32))
            return total + dot(grad, up_chunk(lanes), NT)

        hidden_grad = lax.fori_loop(0, chunks, back, sum_grad)
        unit1, scale1 = unit_v[rows, :], scale_v[rows, 0:1]
        acc[2:3, width : 2 * width] += rows_sum(hidden_grad * unit1)
        acc[2:3, 2 * width : 3 * width] += rows_sum(hidden_grad)
        pre_grad = normalize_grad(hidden_grad * gain1[...], unit1, scale1)
        pre_out[...] = pre_grad
        mixed_grad = pre_grad.astype(BF16)
        mix_g[rows, :] = mixed_grad
        acc[2:3, 0:width] += rows_sum(mixed_grad.astype(F32))
        att_grad = dot(mixed_grad, w_mix[...], NT)
        denom = den[...]
        inverse = 1.0 / jnp.maximum(denom, FLOOR)
        numer = att_grad * inverse
        weighted = att_grad * att[...]
        upper = weighted.astype(BF16)
        lower = (weighted - upper.astype(F32)).astype(BF16)
        square = same_head().astype(BF16)
        factor = inverse * (denom > FLOOR).astype(F32)
        lane = lax.broadcasted_iota(jnp.int32, (1, 128), 1)
        for t in range(width // 128):
            lanes = slice(t * 128, t * 128 + 128)
            summed = dot(upper[:, lanes], square) + dot(lower[:, lanes], square)
            extra = -summed * factor[:, lanes]
            extra = jnp.concatenate([extra[:, 64:128], extra[:, 0:64]], axis=1)
            extra_hi = extra.astype(BF16).astype(F32)
            for head in (0, 1):
                spare = 64 - 64 * head
                both = (
                    numer[:, lanes] * lane_half(head)
                    + extra_hi * (lane == spare).astype(F32)
                    + (extra - extra_hi) * (lane == spare + 1).astype(F32)
                )
                at = t * 256 + head * 128
                given_out[:, at : at + 128] = both.astype(BF16)

    @pl.when(step >= starts[4])
    def _():
        n = step - starts[4]
        lanes = pl.ds(pl.multiple_of(n * chunk, chunk), chunk)
        part = dot(hid_t[...], up_g[:, lanes]).astype(BF16)
        for i in range(chunk // up_w):
            d_up[i // 2, i % 2] = part[:, i * up_w : (i + 1) * up_w].reshape(d_up.shape[2:])

    @pl.when(step == starts[4])
    def _():
        part = dot(att_t[...], mix_g[...]).astype(BF16)
        for c in range(lay.C):
            d_mix[c // 2, c % 2] = part[:, c * mix_w : (c + 1) * mix_w].reshape(d_mix.shape[2:])
        sums[...] = acc[...]


def dense(lay, tokens, att, den, cot, vectors, w_mix, g_up, g_down, mix_shape, split):
    total, width = tokens.shape
    block = 256 if total % 256 == 0 else total
    row_blocks = total // block
    ff = g_up.shape[-1] * lay.C
    chunk = ff // lay.Z
    up_w = g_up.shape[-1]
    slots = [(lay.X, 2, lay.Z, lay.Y) + mix_shape, g_up.shape, g_down.shape]
    if not split:
        g_up = g_up.transpose(2, 3, 4, 0, 1, 5).reshape(lay.Z, lay.Y, g_up.shape[4], ff)
        g_down = g_down.transpose(0, 1, 4, 2, 3, 5).reshape(lay.C, g_down.shape[4], ff)
    starts = [0, row_blocks, 2 * row_blocks, 2 * row_blocks + lay.Z, 3 * row_blocks + lay.Z]
    last = row_blocks - 1
    per = chunk // up_w
    phase = lambda i, n, size: jnp.clip(i - starts[n], 0, size - 1)
    in_phase = lambda n, wide=width: pl.BlockSpec((block, wide), lambda i: (phase(i, n, row_blocks), 0))
    twice = pl.BlockSpec((block, width), lambda i: (jnp.where(i < starts[1], i, phase(i, 3, row_blocks)), 0))
    fixed = lambda shape: pl.BlockSpec(shape, lambda i: (0,) * len(shape), pipeline_mode=pl.Buffered(1))
    anyspace = pl.BlockSpec(memory_space=pl.ANY)
    later = lambda i: phase(i, 4, lay.Z)
    if per == 1:
        up_spec = pl.BlockSpec((1, 1) + slots[1][2:], lambda i: (later(i) // 2, later(i) % 2, 0, 0, 0, 0))
    else:
        up_spec = pl.BlockSpec((per // 2, 2) + slots[1][2:], lambda i: (later(i), 0, 0, 0, 0, 0))
    half = slots[2][:1] + slots[2][2:]
    cuts = pieces(slots[2][4], 1)
    if split:
        down_shape, down_spec = half, anyspace
    else:
        down_shape = slots[2]
        down_spec = pl.BlockSpec(
            slots[2][:2] + (1,) + slots[2][3:], lambda i: (0, 0, phase(i, 2, lay.Z), 0, 0, 0)
        )
    shape = jax.ShapeDtypeStruct
    outs = [
        shape((total, width), BF16),
        shape((total, width), F32),
        shape((total, 2 * width), BF16),
        shape(slots[0], BF16),
        shape(slots[1], BF16),
        shape(down_shape, BF16),
        shape((4, ff), F32),
    ]
    out_specs = [
        in_phase(1), in_phase(3), in_phase(3, 2 * width), fixed(slots[0]), up_spec, down_spec, fixed((4, ff)),
    ]
    scratch = [
        pltpu.VMEM((width, width), BF16),
        pltpu.VMEM((lay.Z, lay.Y, slots[1][4], ff), BF16),
        pltpu.VMEM((lay.C, slots[2][4], ff), BF16),
        pltpu.VMEM((total, ff), BF16),
        pltpu.VMEM((total, ff), BF16),
        pltpu.VMEM((width, total), BF16),
        pltpu.VMEM((width, total), BF16),
        pltpu.VMEM((width, total), BF16),
        pltpu.VMEM((total, width), BF16),
        pltpu.VMEM((total, width), F32),
        pltpu.VMEM((total, 128), F32),
        pltpu.VMEM((total, width), F32),
        pltpu.VMEM((8, ff), F32),
        pltpu.VMEM((4, ff), F32),
        pltpu.SemaphoreType.DMA((3 + lay.C + lay.C * lay.R,)),
    ]
    params = dict(vmem_limit_bytes=VMEM_LIMIT)
    aliases = {}
    if split:
        outs.append(shape(slots[2], BF16))
        out_specs.append(anyspace)
        aliases = {13: 7}
        scratch += [pltpu.VMEM(slots[2], BF16), pltpu.VMEM(half, BF16)]
        for _, n, y_first in cuts:
            tile = (n, slots[2][5])
            first = (lay.Y - 1, lay.X, lay.Z) if y_first else (lay.X - 1, lay.Z, lay.Y)
            scratch.append(pltpu.VMEM(first + tile, BF16))
        scratch += [pltpu.SemaphoreType.DMA((len(cuts) * lay.hops,))] * 4
        params.update(collective_id=2, has_side_effects=True)
    results = pl.pallas_call(
        functools.partial(dense_kernel, lay, row_blocks, chunk, split, cuts),
        grid=(3 * row_blocks + 2 * lay.Z,),
        out_shape=outs,
        in_specs=[in_phase(0), twice, in_phase(3), in_phase(1)] + [fixed(v.shape) for v in vectors] + [anyspace] * 3,
        out_specs=out_specs,
        scratch_shapes=scratch,
        input_output_aliases=aliases,
        compiler_params=pltpu.CompilerParams(**params),
        name="dense",
    )(tokens, att, den, cot, *vectors, w_mix, g_up, g_down)
    return results[:7]


class Scatter:
    def __init__(self, place, source, mine, came, second, third, fourth, target, r0, n, y_first, send, recv, base, fetch):
        self.p, self.source, self.mine, self.came = place, source, mine, came
        self.second, self.third, self.fourth, self.target = second, third, fourth, target
        self.rows, self.r0, self.n, self.y_first = pl.ds(r0, n), r0, n, y_first
        self.send, self.recv, self.base, self.fetch = send, recv, base, fetch

    def stage(self, number):
        p, rows, lay, mine = self.p, self.rows, self.p.lay, self.mine
        first, copies = self.base, []
        if number == 0:
            copies.append(
                (self.source.at[:, 1 - p.k, :, :, rows], self.came.at[:, :, :, rows], p.at(k=1 - p.k))
            )
        elif number == 3:
            first += 1 + lay.X - 1 + lay.Y - 1
            for d, z in enumerate(p.zs()):
                copies.append((mine.at[p.x, z, p.y, rows], self.fourth.at[d], p.at(z=z)))
        else:
            along_y = (number == 1) == self.y_first
            landing = self.second if number == 1 else self.third
            first += 1
            if number == 2:
                first += (lay.Y - 1) if self.y_first else (lay.X - 1)
            for d, other in enumerate(p.ys() if along_y else p.xs()):
                if along_y:
                    part = mine.at[:, :, other, rows] if number == 1 else mine.at[p.x, :, other, rows]
                    copies.append((part, landing.at[d], p.at(y=other)))
                else:
                    part = mine.at[other, :, :, rows] if number == 1 else mine.at[other, :, p.y, rows]
                    copies.append((part, landing.at[d], p.at(x=other)))
        return [
            remote(src, dst, self.send.at[first + i], self.recv.at[first + i], device)
            for i, (src, dst, device) in enumerate(copies)
        ]

    def own_copy(self):
        return pltpu.make_async_copy(
            self.source.at[:, self.p.k, :, :, self.rows], self.mine.at[:, :, :, self.rows], self.fetch
        )

    def start(self, number):
        for copy in self.stage(number):
            copy.start()

    def begin(self):
        self.start(0)
        if self.fetch is not None:
            self.own_copy().start()

    def advance(self, number):
        self.add(number)
        if number < 4:
            self.start(number)

    def add(self, number):
        p, rows, lay, mine = self.p, self.rows, self.p.lay, self.mine
        if number == 1 and self.fetch is not None:
            self.own_copy().wait()
        for copy in self.stage(number - 1):
            copy.wait_recv()
        if number == 1:

            def add(i, _):
                x, zy = i // (lay.Z * lay.Y), i % (lay.Z * lay.Y)
                z, y = zy // lay.Y, zy % lay.Y
                mine[x, z, y, rows] = (
                    mine[x, z, y, rows].astype(F32) + self.came[x, z, y, rows].astype(F32)
                ).astype(BF16)
                return 0

            lax.fori_loop(0, lay.X * lay.Z * lay.Y, add, 0)
        elif number == 2:
            outer = lay.X if self.y_first else lay.Z
            inner = lay.Z if self.y_first else lay.Y

            def add(i, _):
                a, b = i // inner, i % inner
                total = jnp.zeros((self.n, mine.shape[-1]), F32)
                for d in range(self.second.shape[0]):
                    total = total + self.second[d, a, b].astype(F32)
                if self.y_first:
                    mine[a, b, p.y, rows] = (mine[a, b, p.y, rows].astype(F32) + total).astype(BF16)
                else:
                    mine[p.x, a, b, rows] = (mine[p.x, a, b, rows].astype(F32) + total).astype(BF16)
                return 0

            lax.fori_loop(0, outer * inner, add, 0)
        elif number == 3:

            def add(z, _):
                total = mine[p.x, z, p.y, rows].astype(F32)
                for d in range(self.third.shape[0]):
                    total = total + self.third[d, z].astype(F32)
                mine[p.x, z, p.y, rows] = total.astype(BF16)
                return 0

            lax.fori_loop(0, lay.Z, add, 0)
        else:
            total = mine[p.x, p.z, p.y, rows].astype(F32)
            for d in range(lay.Z - 1):
                total = total + self.fourth[d].astype(F32)
            self.target[rows, :] = total

    def sent(self, numbers):
        for number in numbers:
            for copy in self.stage(number):
                copy.wait_send()


def backward_kernel(
    lay, seqs, length, cuts, split, *refs
):
    (carry, ids, prev, tok_t, sums, q_hbm, k_hbm, v_hbm, given_hbm, full_in, pre, d_mix, d_up, d_down) = refs[:14]
    (tokens_grad, o_in, o_mix, o_up, o_down, o_sums) = refs[14:20]
    rest = list(refs[20:])
    (mask, tab, out_state, in_state, flags, key_part, value_part, grads, held, given_in, d_in, vec, vec_in,
     mine_mix, mine_up, mine_down, came_mix, came_up, came_in) = rest[:19]
    send, recv, misc_send, misc_recv, local = rest[-5:]
    came_down = None if split else rest[19]
    landing = rest[19 if split else 20 : -5]
    p = Place(lay)
    _, total_rows, width = held.shape
    q_in, k_in, v_in = held.at[0], held.at[1], held.at[2]
    pairs = width // 128
    total = seqs * pairs
    spot = local.shape[0] - 4
    loads = [
        pltpu.make_async_copy(src, dst, local.at[spot + i])
        for i, (src, dst) in enumerate(((q_hbm, q_in), (k_hbm, k_in), (v_hbm, v_in), (given_hbm, given_in)))
    ]
    for copy in loads:
        copy.start()
    p.barrier()

    groups, base, used = [], 0, 0
    for index, (source, mine, came, target, parts) in enumerate(
        (
            (d_down, mine_down, came_down, o_down, cuts[0]),
            (d_up, mine_up, came_up, o_up, cuts[1]),
            (d_mix, mine_mix, came_mix, o_mix, cuts[2]),
            (d_in, d_in.at[:, p.k], came_in, o_in, cuts[3]),
        )
    ):
        group = []
        for r0, n, y_first in parts:
            second, third, fourth = landing[3 * used : 3 * used + 3]
            fetch = local.at[used] if index < 3 else None
            group.append(
                Scatter(p, source, mine, came, second, third, fourth, target, r0, n, y_first, send, recv, base, fetch)
            )
            base += lay.hops
            used += 1
        groups.append(group)
    if split:
        down_copy = pltpu.make_async_copy(d_down, mine_down, local.at[0])
        down_copy.start()
    for group in groups[1 if split else 0 : 3]:
        for flow in group:
            flow.begin()
    if split:
        down_copy.wait()
        for flow in groups[0]:
            flow.start(2)

    def pre_copy(b):
        return pltpu.make_async_copy(pre.at[pl.ds(b * 256, 256)], key_part.at[pl.ds(b * 256, 256)], misc_recv.at[2 + b])

    def grad_copy(b):
        return pltpu.make_async_copy(value_part.at[pl.ds(b * 256, 256)], tokens_grad.at[pl.ds(b * 256, 256)], misc_send.at[2 + b])

    blocks = total_rows // 256

    cos_a, sin_a, _, _ = angle_tables(length)
    cos_e, sin_e = edge_angles(cos_a, sin_a, length)
    for s in range(seqs):
        _, _, carried, last_mask, passes = seq_masks(ids, prev, s, length, p.c > 0)
        tab[s, 0] = cos_a * carried
        tab[s, 1] = sin_a * carried
        tab[s, 2] = cos_e * last_mask
        tab[s, 3] = sin_e * last_mask
        flags[s] = jnp.broadcast_to(passes, (8, 256))
    for copy in loads:
        copy.wait()

    def where(it):
        s, pair = it // pairs, it % pairs
        return s, pl.ds(pl.multiple_of(s * length, length), length), pl.ds(pl.multiple_of(pair * 128, 128), 128)

    def given_of(it):
        s, pair = it // pairs, it % pairs
        rows = pl.ds(pl.multiple_of(s * length, length), length)
        lane = lax.broadcasted_iota(jnp.int32, (1, 128), 1)
        plus = [given_in[rows, pl.ds(pl.multiple_of(pair * 256 + 128 * head, 128), 128)] for head in (0, 1)]
        given = plus[0] * lane_half(0).astype(BF16) + plus[1] * lane_half(1).astype(BF16)
        extra = jnp.zeros((length, 128), F32)
        for head in (0, 1):
            spare = 64 - 64 * head
            own = ((lane == spare) | (lane == spare + 1)).astype(F32)
            one = jnp.sum(plus[head].astype(F32) * own, axis=1, keepdims=True)
            extra = extra + one * lane_half(head)
        return plus, given, extra

    def local_state(it, _):
        s, rows, lanes = where(it)
        _, given, extra = given_of(it)
        queries, given = q_in[rows, lanes], given.astype(F32)
        scaled = jnp.concatenate([given * tab[s, 0], given * tab[s, 1]], axis=1).astype(BF16)
        state = dot(queries, scaled, TN)
        wide = queries.astype(F32) * extra
        for part in (0, 1):
            packed = pack_state(state[:, part * 128 : part * 128 + 128])
            out_state[it, 0:64, part * 128 : part * 128 + 128] = packed.astype(BF16)
            total_row = jnp.sum(wide * tab[s, part], axis=0, keepdims=True)
            out_state[it, 64:80, part * 128 : part * 128 + 128] = jnp.broadcast_to(total_row, (16, 128)).astype(BF16)
        return 0

    lax.fori_loop(0, total, local_state, 0)

    def chain_copy():
        return remote(out_state, in_state, misc_send.at[1], misc_recv.at[1], p.ring(-1))

    turn_c, turn_s = math.cos(OMEGA * length), math.sin(OMEGA * length)

    def hand_on():
        def one(it, _):
            came = in_state[it].astype(F32)
            came_c, came_s = came[:, 0:128], came[:, 128:256]
            turned = jnp.concatenate(
                [came_c * turn_c - came_s * turn_s, came_c * turn_s + came_s * turn_c], axis=1
            )
            state = out_state[it].astype(F32) + flags[it // pairs, 0:1, :] * turned
            out_state[it] = state.astype(BF16)
            return 0

        lax.fori_loop(0, total, one, 0)

    def chain_step():
        @pl.when(p.c == lay.C - 1)
        def _():
            in_state[...] = jnp.zeros_like(in_state)

        @pl.when(p.c < lay.C - 1)
        def _():
            chain_copy().wait_recv()
            hand_on()

        @pl.when(p.c > 0)
        def _():
            chain_copy().start()

    def onward(number, group):
        for flow in groups[group]:
            flow.advance(number)

    back = lay.C - 1 - p.c
    pl.when(back == 0)(chain_step)
    pl.when(back == 1)(chain_step)
    for group in (1, 2) if split else (0, 1):
        onward(1, group)
    chain_turn = (total * 2) // 3 + ((back - 2) * (total // 3)) // max(lay.C - 2, 1)

    during = [(1, 3, 0), (7, 2, 1), (9, 2, 2), (10, 4, 0)] if split else [(0, 1, 2), (3, 2, 0), (7, 2, 1), (9, 3, 0)]
    block = 256 if length % 256 == 0 else length

    def local_attention(it, _):
        @pl.when((it == chain_turn) & (back > 1))
        def _():
            chain_step()

        for turn, number, group in during:

            @pl.when(it == (turn * total) // 12)
            def _(number=number, group=group):
                onward(number, group)

        s, rows, lanes = where(it)
        for seq in range(seqs):

            @pl.when(it == seq * pairs)
            def _(seq=seq):
                row, column, _, _, _ = seq_masks(ids, prev, seq, length, p.c > 0)
                at_j = lax.broadcasted_iota(jnp.int32, (length, length), 0)
                at_i = lax.broadcasted_iota(jnp.int32, (length, length), 1)
                allowed = (column[:, 0:1] == row) & (at_j <= at_i)
                cos_a, sin_a, cos_r, sin_r = angle_tables(length)
                mask[...] = jnp.where(allowed, cos_a[:, 0:1] * cos_r + sin_a[:, 0:1] * sin_r, 0.0)

        lane = lax.broadcasted_iota(jnp.int32, (1, 128), 1)
        queries, keys, values = q_in[rows, lanes], k_in[rows, lanes], v_in[rows, lanes]
        plus, given, extra = given_of(it)
        query_total = jnp.zeros((length, 128), F32)
        for head in (0, 1):
            side = lane_half(head)
            only = side.astype(BF16)
            spare = 64 - 64 * head
            given_plus = plus[head]
            ones = ((lane == spare) | (lane == spare + 1)).astype(BF16)
            value_plus = values * only + ones
            key_only, query_only, given_only = keys * only, queries * only, given * only
            query_parts = []
            for b in range(length // block):
                lo = b * block
                scores = dot(key_only[lo : lo + block], queries[lo:], NT) * mask[lo : lo + block, lo:]
                grads_ji = (
                    dot(value_plus[lo : lo + block], given_plus[lo:], NT) * mask[lo : lo + block, lo:]
                ).astype(BF16)
                here = pl.ds(pl.multiple_of(s * length + lo, block), block)
                key_add = dot(grads_ji, query_only[lo:])
                value_add = dot(scores.astype(BF16), given_only[lo:])
                if head == 0:
                    key_part[here, lanes] = key_add
                    value_part[here, lanes] = value_add
                else:
                    key_part[here, lanes] += key_add
                    value_part[here, lanes] += value_add
                add = dot(grads_ji, key_only[lo : lo + block], TN)
                if lo:
                    query_total = jnp.concatenate([query_total[:lo], query_total[lo:] + add], axis=0)
                else:
                    query_total = query_total + add
        state_c, state_s = unpack_state(carry[it])
        wide = jnp.concatenate([state_c, state_s], axis=0).astype(BF16)
        reach = dot(given, wide, NT)
        totals = carry[it, 64:80, :].astype(F32)[0:1]
        query_total = query_total + tab[s, 0] * (reach[:, 0:128] + extra * totals[:, 0:128])
        query_total = query_total + tab[s, 1] * (reach[:, 128:256] + extra * totals[:, 128:256])
        grads[rows, lanes] = jnp.where(queries.astype(F32) > 0.0, query_total, 0.0).astype(BF16)
        return 0

    lax.fori_loop(0, total, local_attention, 0)

    def finish(it, _):
        s, rows, lanes = where(it)
        pair = it % pairs
        keys, values = k_in[rows, lanes], v_in[rows, lanes]
        state_c, state_s = unpack_state(in_state[it])
        by_row = jnp.concatenate([state_c, state_s], axis=0).astype(BF16)
        by_lane = jnp.concatenate([state_c, state_s], axis=1).astype(BF16)
        totals = in_state[it, 64:80, :].astype(F32)[0:1]
        c_j, s_j = tab[s, 2], tab[s, 3]
        key_reach = dot(values, by_row, NT) + totals
        value_reach = dot(keys, by_lane)
        key_grad = key_part[rows, lanes] + c_j * key_reach[:, 0:128] + s_j * key_reach[:, 128:256]
        value_grad = value_part[rows, lanes] + c_j * value_reach[:, 0:128] + s_j * value_reach[:, 128:256]
        key_lanes = pl.ds(pl.multiple_of(width + pair * 128, 128), 128)
        value_lanes = pl.ds(pl.multiple_of(2 * width + pair * 128, 128), 128)
        grads[rows, key_lanes] = jnp.where(keys.astype(F32) > 0.0, key_grad, 0.0).astype(BF16)
        grads[rows, value_lanes] = value_grad.astype(BF16)
        return 0

    lax.fori_loop(0, total, finish, 0)
    for number, group in [(3, 1), (3, 2)] if split else [(2, 2), (4, 0), (3, 1), (3, 2)]:
        onward(number, group)
    for b in range(blocks):
        pre_copy(b).start()
    thirds = [
        pltpu.make_async_copy(
            full_in.at[:, pl.ds(i * width, width)], held.at[i, pl.ds(0, width)], local.at[spot + i]
        )
        for i in range(3)
    ]
    for copy in thirds:
        copy.start()
    vec[0] = sums[...]

    def bias_sum(n, _):
        lanes = pl.ds(pl.multiple_of(n * 256, 256), 256)
        vec[0, 1:2, lanes] = rows_sum(grads[:, lanes].astype(F32))
        return 0

    lax.fori_loop(0, 3 * width // 256, bias_sum, 0)

    in_a, in_w = o_in.shape
    piece = math.lcm(in_w, 128)
    for n in range(3 * width // piece):
        for m in range(width // 256):
            part = dot(tok_t[m * 256 : (m + 1) * 256, :], grads[:, n * piece : (n + 1) * piece]).astype(BF16)
            for i in range(piece // in_w):
                c = n * (piece // in_w) + i
                lo = m * 256
                while lo < (m + 1) * 256:
                    r = lo // in_a
                    hi = min((r + 1) * in_a, (m + 1) * 256)
                    d_in[c // 2, c % 2, r // lay.Y, r % lay.Y, lo - r * in_a : hi - r * in_a, :] = part[
                        lo - m * 256 : hi - m * 256, i * in_w : (i + 1) * in_w
                    ]
                    lo = hi
    for flow in groups[3]:
        flow.begin()

    def vector_stage(number):
        first = (0, 1, lay.X, lay.X + lay.Y - 1)[number]
        peers = (
            [p.at(k=1 - p.k)],
            [p.at(x=x) for x in p.xs()],
            [p.at(y=y) for y in p.ys()],
            [p.at(z=z) for z in p.zs()],
        )[number]
        shift = 2 + blocks + first
        return [
            remote(vec.at[number], vec_in.at[first + i], misc_send.at[shift + i], misc_recv.at[shift + i], peer)
            for i, peer in enumerate(peers)
        ]

    def vector_start(number):
        for copy in vector_stage(number):
            copy.start()

    def vector_add(number):
        total_vec = vec[number]
        first = (0, 1, lay.X, lay.X + lay.Y - 1)[number]
        for i, copy in enumerate(vector_stage(number)):
            copy.wait_recv()
            total_vec = total_vec + vec_in[first + i]
        if number == 3:
            o_sums[...] = total_vec
        else:
            vec[number + 1] = total_vec
            vector_start(number + 1)

    vector_start(0)
    for copy in thirds:
        copy.wait()
    after = [[(1, 3)], [(4, 1), (4, 2)], [], []]
    for b in range(blocks):
        pre_copy(b).wait()
        part = slice(b * 256, (b + 1) * 256)
        out = key_part[part, :]
        for i in range(3):
            out = out + dot(grads[part, i * width : (i + 1) * width], held[i, 0:width, :], NT)
        value_part[part, :] = out
        grad_copy(b).start()
        for number, group in after[b] if b < len(after) else []:
            onward(number, group)
    vector_add(0)
    onward(2, 3)
    vector_add(1)
    onward(3, 3)
    vector_add(2)
    onward(4, 3)
    vector_add(3)
    for b in range(blocks):
        grad_copy(b).wait()
    for group in groups:
        for flow in group:
            flow.sent(range(2, 4) if split and group is groups[0] else range(4))
    for number in range(4):
        for copy in vector_stage(number):
            copy.wait_send()

    @pl.when(p.c > 0)
    def _():
        chain_copy().wait_send()


def backward(
    lay, ids, prev, q, k, v, given, carry, tok_t, full_in, sums, pre, d_mix, d_up, d_down, shapes, split
):
    seqs, length = ids.shape
    rows, width = q.shape
    total = seqs * (width // 128)
    slots = [(lay.X, 2, lay.Z, lay.Y) + s for s in shapes]
    in_slots = slots[3]
    cuts = tuple(pieces(s[4], n) for s, n in zip(slots, (1, 1, 1, 3), strict=True))
    landing = []
    for index, (slot, parts) in enumerate(zip(slots, cuts, strict=True)):
        for _, n, y_first in parts:
            tile = (n, slot[5])
            if split and index == 0:
                landing += [(1, 1, 1, 16, 128), ((lay.X if y_first else lay.Y) - 1, lay.Z) + tile]
            elif y_first:
                landing += [(lay.Y - 1, lay.X, lay.Z) + tile, (lay.X - 1, lay.Z) + tile]
            else:
                landing += [(lay.X - 1, lay.Z, lay.Y) + tile, (lay.Y - 1, lay.Z) + tile]
            landing.append((lay.Z - 1,) + tile)
    flows = sum(len(c) for c in cuts)
    vmem, anyspace = pl.BlockSpec(memory_space=pltpu.VMEM), pl.BlockSpec(memory_space=pl.ANY)
    shape = jax.ShapeDtypeStruct
    ff = sums.shape[1]
    blocks = rows // 256
    half = [(s[0],) + s[2:] for s in slots]
    hop = lay.hops
    misc = 2 + blocks + hop
    scratch = [
        pltpu.VMEM((length, length), F32),
        pltpu.VMEM((seqs, 4, length, 128), F32),
        pltpu.VMEM((total, 80, 256), BF16),
        pltpu.VMEM((total, 80, 256), BF16),
        pltpu.VMEM((seqs, 8, 256), F32),
        pltpu.VMEM((rows, width), F32),
        pltpu.VMEM((rows, width), F32),
        pltpu.VMEM((rows, 3 * width), BF16),
        pltpu.VMEM((3, rows, width), BF16),
        pltpu.VMEM((rows, 2 * width), BF16),
        pltpu.VMEM(in_slots, BF16),
        pltpu.VMEM((4, 4, ff), F32),
        pltpu.VMEM((hop, 4, ff), F32),
    ]
    scratch += [pltpu.VMEM(half[i], BF16) for i in (2, 1, 0)] + [pltpu.VMEM(half[i], BF16) for i in ((2, 1, 3) if split else (2, 1, 3, 0))]
    scratch += [pltpu.VMEM(s, BF16) for s in landing]
    scratch += [
        pltpu.SemaphoreType.DMA((flows * hop,)),
        pltpu.SemaphoreType.DMA((flows * hop,)),
        pltpu.SemaphoreType.DMA((misc,)),
        pltpu.SemaphoreType.DMA((misc,)),
        pltpu.SemaphoreType.DMA((flows + 4,)),
    ]
    return pl.pallas_call(
        functools.partial(backward_kernel, lay, seqs, length, cuts, split),
        out_shape=[shape((rows, width), F32)]
        + [shape(slots[i][4:], F32) for i in (3, 2, 1, 0)]
        + [shape((4, ff), F32)],
        in_specs=[vmem] * 5 + [anyspace] * 9,
        out_specs=[anyspace] + [vmem] * 5,
        scratch_shapes=scratch,
        compiler_params=pltpu.CompilerParams(
            collective_id=1, has_side_effects=True, vmem_limit_bytes=VMEM_LIMIT
        ),
        name="backward_attention",
    )(carry, ids, prev, tok_t, sums, q, k, v, given, full_in, pre, d_mix, d_up, d_down)


def finish_kernel(tok_in, layer_in, in_in, mix_in, up_in, down_in, sums, *outs):
    layer_out, tokens_grad, o_in, in_b, o_mix, mix_b, gain1, shift1, o_up, up_b, o_down, down_b, gain2, shift2 = outs
    width = tok_in.shape[1]
    layer_out[...] = layer_in[...]
    tokens_grad[...] = tok_in[...]

    @pl.when(pl.program_id(0) == 0)
    def _():
        o_in[...] = in_in[...]
        o_mix[...] = mix_in[...]
        o_up[...] = up_in[...]
        o_down[...] = jnp.transpose(down_in[...])
        for out, row, at in (
            (up_b, 0, 0), (in_b, 1, 0), (mix_b, 2, 0), (gain1, 2, 1), (shift1, 2, 2), (down_b, 2, 3), (gain2, 3, 0), (shift2, 3, 1),
        ):
            size = out.shape[0]
            out[...] = sums[row : row + 1, at * width : at * width + size].reshape(size)


def finish_all(tokens_grad, layer_out, o_in, o_mix, o_up, o_down, sums):
    rows, width = tokens_grad.shape
    ff = sums.shape[1]
    block = 256 if rows % 256 == 0 else rows
    by_row = pl.BlockSpec((block, width), lambda i: (i, 0))
    fixed = lambda shape: pl.BlockSpec(shape, lambda i: (0,) * len(shape))
    sizes = [
        None, None, o_in.shape, (3 * width,), o_mix.shape, (width,), (width,), (width,), o_up.shape, (ff,),
        o_down.shape[::-1], (width,), (width,), (width,),
    ]
    shape = jax.ShapeDtypeStruct
    return pl.pallas_call(
        finish_kernel,
        grid=(rows // block,),
        out_shape=[shape((rows, width), BF16), shape((rows, width), F32)] + [shape(n, F32) for n in sizes[2:]],
        in_specs=[by_row] * 2 + [fixed(a.shape) for a in (o_in, o_mix, o_up, o_down, sums)],
        out_specs=[by_row] * 2 + [fixed(n) for n in sizes[2:]],
        name="finish",
    )(tokens_grad, layer_out, o_in, o_mix, o_up, o_down, sums)


def per_device(
    tokens, segment_ids, in_weight, in_bias, mix_weight, mix_bias, first_gain, first_shift,
    up_weight, up_bias, down_weight, down_bias, second_gain, second_shift, cotangent,
):
    lay = Layout(lax.axis_size("row"), lax.axis_size("col"))
    seqs, length, width = tokens.shape
    flat = tokens.reshape(seqs * length, width)
    split = up_weight.shape[1] % 128 == 0 and down_weight.shape[0] % 128 == 0
    shards = (in_weight, mix_weight, up_weight, down_weight.T)
    att, den, carry, prev, q, k, v, full_in, full_mix, tok_t, g_up, g_down = forward(
        lay, flat, segment_ids, in_bias, shards, split
    )
    vectors = (up_bias, mix_bias, down_bias, first_gain, first_shift, second_gain, second_shift)
    layer_out, pre, given, d_mix, d_up, d_down, sums = dense(
        lay, flat, att, den, cotangent.reshape(seqs * length, width), vectors, full_mix, g_up, g_down,
        mix_weight.shape, split,
    )
    tokens_grad, o_in, o_mix, o_up, o_down, o_sums = backward(
        lay, segment_ids, prev, q, k, v, given, carry, tok_t, full_in, sums, pre, d_mix, d_up, d_down,
        [shards[i].shape for i in (3, 2, 1, 0)], split,
    )
    outs = finish_all(tokens_grad, layer_out, o_in, o_mix, o_up, o_down, o_sums)
    return (outs[0].reshape(tokens.shape), outs[1].reshape(tokens.shape), *outs[2:])


def solution(mesh):
    block, matrix, rep = P("row", "col", None), P("row", "col"), P()
    return jax.shard_map(
        per_device,
        mesh=mesh,
        in_specs=(block, matrix, matrix, rep, matrix, rep, rep, rep, matrix, rep, matrix, rep, rep, rep, block),
        out_specs=(block, block, matrix, rep, matrix, rep, rep, rep, matrix, rep, matrix, rep, rep, rep),
        check_vma=False,
    )
```

```python
import functools
import math

import jax
import jax.numpy as jnp
from jax import lax
from jax.experimental import pallas as pl
from jax.experimental.pallas import tpu as pltpu
from jax.sharding import PartitionSpec as P

HEADS = 12
HEAD_DIM = 64
DOC_MAX = 2000
EPSILON = 1e-05
FLOOR = 4.0
OMEGA = math.pi / (2.0 * DOC_MAX)
MESH = pl.DeviceIdType.MESH
F32 = jnp.float32
BF16 = jnp.bfloat16
VMEM_LIMIT = 67_043_328

NN = (((1,), (0,)), ((), ()))
NT = (((1,), (1,)), ((), ()))
TN = (((0,), (0,)), ((), ()))


def dot(first, second, dims=NN):
    return lax.dot_general(first, second, dims, preferred_element_type=F32)


class Layout:
    def __init__(self, rows, cols):
        self.R, self.C = rows, cols
        self.Z = 4 if rows % 4 == 0 else rows
        self.Y = rows // self.Z
        self.K = 2
        self.X = cols // 2
        self.hops = (self.Z - 1) + (self.Y - 1) + (self.X - 1) + 1


class Place:
    def __init__(self, lay):
        self.lay = lay
        self.r = lax.axis_index("row")
        self.c = lax.axis_index("col")
        self.z, self.y = self.r // lay.Y, self.r % lay.Y
        self.x, self.k = self.c // 2, self.c % 2

    def at(self, z=None, y=None, x=None, k=None):
        z = self.z if z is None else z
        y = self.y if y is None else y
        x = self.x if x is None else x
        k = self.k if k is None else k
        return {"row": z * self.lay.Y + y, "col": x * 2 + k}

    def zs(self):
        return [lax.rem(self.z + d, self.lay.Z) for d in range(1, self.lay.Z)]

    def ys(self):
        return [lax.rem(self.y + d, self.lay.Y) for d in range(1, self.lay.Y)]

    def xs(self):
        return [lax.rem(self.x + d, self.lay.X) for d in range(1, self.lay.X)]

    def ring(self, step):
        return {"row": self.r, "col": lax.rem(self.c + step + self.lay.C, self.lay.C)}

    def barrier(self):
        peers = [self.at(z=z) for z in self.zs()] + [self.at(y=y) for y in self.ys()]
        peers += [self.at(x=x) for x in self.xs()] + [self.at(k=1 - self.k)]
        peers += [self.ring(1), self.ring(-1)]
        sem = pltpu.get_barrier_semaphore()
        for peer in peers:
            pl.semaphore_signal(sem, inc=1, device_id=peer, device_id_type=MESH)
        pl.semaphore_wait(sem, len(peers))


def remote(src, dst, send, recv, device):
    return pltpu.make_async_remote_copy(
        src_ref=src, dst_ref=dst, send_sem=send, recv_sem=recv, device_id=device, device_id_type=MESH
    )


class Gather:
    def __init__(self, place, shard, whole, r0, n, y_first, send, recv, base):
        self.p, self.shard, self.whole = place, shard, whole
        self.rows = pl.ds(r0, n)
        self.y_first = y_first
        self.send, self.recv, self.base = send, recv, base

    def stage(self, number):
        p, g, rows, lay = self.p, self.whole, self.rows, self.p.lay
        first, copies = self.base, []
        if number == 0:
            for z in p.zs():
                copies.append((self.shard.at[rows], g.at[p.x, p.k, p.z, p.y, rows], p.at(z=z)))
        else:
            first += lay.Z - 1
            along_y = (number == 1) == self.y_first
            if number == 3:
                part = g.at[:, p.k, :, :, rows]
                copies.append((part, part, p.at(k=1 - p.k)))
                first += lay.Y - 1 + lay.X - 1
            else:
                if number == 2:
                    first += (lay.Y - 1) if self.y_first else (lay.X - 1)
                    part = g.at[:, p.k, :, p.y, rows] if along_y else g.at[p.x, p.k, :, :, rows]
                else:
                    part = g.at[p.x, p.k, :, p.y, rows]
                for peer in [p.at(y=y) for y in p.ys()] if along_y else [p.at(x=x) for x in p.xs()]:
                    copies.append((part, part, peer))
        return [
            remote(src, dst, self.send.at[first + i], self.recv.at[first + i], device)
            for i, (src, dst, device) in enumerate(copies)
        ]

    def start(self, number):
        for copy in self.stage(number):
            copy.start()

    def arrive(self, number):
        for copy in self.stage(number):
            copy.wait_recv()

    def advance(self, number):
        self.arrive(number - 1)
        self.start(number)

    def sent(self, numbers):
        for number in numbers:
            for copy in self.stage(number):
                copy.wait_send()


def pieces(rows, count):
    tiles, many = rows // 16, 2 * count
    many = min(many, tiles)
    cuts = [(tiles * i + many - 1) // many for i in range(many + 1)]
    return [(cuts[i] * 16, (cuts[i + 1] - cuts[i]) * 16, i % 2 == 1) for i in range(many)]


def lane_half(head):
    lane = lax.broadcasted_iota(jnp.int32, (1, 128), 1)
    return ((lane < 64) if head == 0 else (lane >= 64)).astype(F32)


def same_head():
    row = lax.broadcasted_iota(jnp.int32, (128, 128), 0)
    lane = lax.broadcasted_iota(jnp.int32, (128, 128), 1)
    return ((row < 64) == (lane < 64)).astype(F32)


def seq_masks(ids_ref, prev_ref, seq, length, has_prev):
    row = ids_ref[seq : seq + 1, :].astype(F32)
    column = jnp.transpose(jnp.broadcast_to(row, (128, length)))
    lane = lax.broadcasted_iota(jnp.int32, (1, length), 1)
    first = jnp.sum(jnp.where(lane == 0, row, 0.0), axis=1, keepdims=True)
    last = jnp.sum(jnp.where(lane == length - 1, row, 0.0), axis=1, keepdims=True)
    before = prev_ref[seq : seq + 1, :].astype(F32)
    before = jnp.sum(jnp.where(lane == length - 1, before, 0.0), axis=1, keepdims=True)
    before = jnp.where(has_prev, before, -1.0)
    carry = (column == before).astype(F32)
    last_mask = (column == last).astype(F32)
    passes = ((first == last) & (first == before)).astype(F32)
    return row, column, carry, last_mask, passes


def angle_tables(length):
    row = lax.broadcasted_iota(jnp.int32, (1, length), 1).astype(F32) * OMEGA
    rows = jnp.cos(row), jnp.sin(row)
    return *(jnp.transpose(jnp.broadcast_to(r, (128, length))) for r in rows), *rows


def edge_angles(cosine, sine, length):
    turn_c, turn_s = math.cos(OMEGA * length), math.sin(OMEGA * length)
    return cosine * turn_c + sine * turn_s, sine * turn_c - cosine * turn_s


def unpack_state(block):
    low, high = lane_half(0), lane_half(1)
    out = []
    for half in (0, 1):
        part = block[0:64, half * 128 : half * 128 + 128].astype(F32)
        out.append(jnp.concatenate([part * low, part * high], axis=0))
    return out


def pack_state(square):
    square = square * same_head()
    return square[0:64] + square[64:128]


def unslot(whole, flat, lay, a, b, transposed):
    for c in range(lay.C):
        if transposed:
            for r in range(lay.R):
                flat[c * a : (c + 1) * a, r * b : (r + 1) * b] = whole[
                    c // 2, c % 2, r // lay.Y, r % lay.Y
                ]
        else:
            for z in range(lay.Z):
                for y in range(lay.Y):
                    r = z * lay.Y + y
                    flat[r * a : (r + 1) * a, c * b : (c + 1) * b] = whole[c // 2, c % 2, z, y]


def forward_kernel(
    lay, seqs, length, cuts, split,
    tokens, ids, bias_in, in_s, mix_s, up_s, down_s,
    att, den, carry, prev, q_hbm, k_hbm, v_hbm, in_hbm, mix_hbm, tok_hbm, g_up, g_down,
    q_out, k_out, v_out, full_in, full_mix, tok_t, g_in, g_mix, bias, mask, tab, out_state, flags,
    send, recv, misc_send, misc_recv, local,
):
    p = Place(lay)
    pairs = q_out.shape[1] // 128
    width = q_out.shape[1]
    total = seqs * pairs
    outputs = [
        pltpu.make_async_copy(src, dst, local.at[4 + i])
        for i, (src, dst) in enumerate(
            ((q_out, q_hbm), (k_out, k_hbm), (v_out, v_hbm), (full_in, in_hbm), (tok_t, tok_hbm), (full_mix, mix_hbm))
        )
    ]
    p.barrier()
    flows = []
    base = 0
    groups = []
    for shard, whole, parts in zip(
        (in_s, mix_s, up_s, down_s), (g_in, g_mix, g_up, g_down), cuts, strict=True
    ):
        group = []
        for r0, n, y_first in parts:
            group.append(Gather(p, shard, whole, r0, n, y_first, send, recv, base))
            base += lay.hops
        groups.append(group)
        flows += group
    own = [
        pltpu.make_async_copy(shard, whole.at[p.x, p.k, p.z, p.y], local.at[i])
        for i, (shard, whole) in enumerate(
            zip((in_s, mix_s, up_s, down_s), (g_in, g_mix, g_up, g_down), strict=True)
        )
    ]
    for copy in own:
        copy.start()
    ring_ids = remote(ids, prev, misc_send.at[0], misc_recv.at[0], p.ring(1))
    ring_ids.start()
    for flow in flows:
        flow.start(0)
    for copy in own:
        copy.wait()
    for flow in groups[0]:
        flow.advance(1)
    tok_t[...] = jnp.transpose(tokens[...])
    bias[...] = bias_in[...].astype(F32).reshape(bias.shape)
    outputs[4].start()

    cos_a, sin_a, cos_r, sin_r = angle_tables(length)
    cos_e, sin_e = edge_angles(cos_a, sin_a, length)
    ring_ids.wait_recv()
    for s in range(seqs):
        row, column, carried, last_mask, passes = seq_masks(ids, prev, s, length, p.c > 0)
        at_i = lax.broadcasted_iota(jnp.int32, (length, length), 0)
        at_j = lax.broadcasted_iota(jnp.int32, (length, length), 1)
        allowed = (column[:, 0:1] == row) & (at_j <= at_i)
        mask[s] = jnp.where(allowed, cos_a[:, 0:1] * cos_r + sin_a[:, 0:1] * sin_r, 0.0)
        tab[s, 0] = cos_a * carried
        tab[s, 1] = sin_a * carried
        tab[s, 2] = cos_e * last_mask
        tab[s, 3] = sin_e * last_mask
        flags[s] = jnp.broadcast_to(passes, (8, 256))

    def go(number, some):
        for flow in some:
            flow.advance(number)

    ins, mixes, ups, downs = groups
    go(2, ins)
    go(1, mixes)
    go(3, ins)
    go(1, ups[:2])
    for flow in ins:
        flow.arrive(3)
    go(2, mixes)
    unslot(g_in, full_in, lay, in_s.shape[0], in_s.shape[1], False)
    outputs[3].start()
    half = tokens.shape[0] // 2

    def project(target, start, relu):
        for m in range(2):
            rows = slice(m * half, (m + 1) * half)
            out = dot(tokens[rows, :], full_in[:, start : start + width]) + bias[:, start : start + width]
            if relu:
                out = jnp.maximum(out, 0.0)
            target[rows, :] = out.astype(BF16)

    project(k_out, width, True)
    go(1, ups[2:])
    go(2, ups[:2])
    project(v_out, 2 * width, False)

    def where(it):
        s, pair = it // pairs, it % pairs
        return s, pl.ds(pl.multiple_of(s * length, length), length), pl.ds(pl.multiple_of(pair * 128, 128), 128)

    def local_state(it, _):
        s, rows, lanes = where(it)
        keys, values = k_out[rows, lanes], v_out[rows, lanes].astype(F32)
        scaled = jnp.concatenate([values * tab[s, 2], values * tab[s, 3]], axis=1).astype(BF16)
        state = dot(keys, scaled, TN)
        wide = keys.astype(F32)
        for part in (0, 1):
            packed = pack_state(state[:, part * 128 : part * 128 + 128])
            out_state[it, 0:64, part * 128 : part * 128 + 128] = packed.astype(BF16)
            total_row = jnp.sum(wide * tab[s, 2 + part], axis=0, keepdims=True)
            out_state[it, 64:80, part * 128 : part * 128 + 128] = jnp.broadcast_to(total_row, (16, 128)).astype(BF16)
        return 0

    lax.fori_loop(0, total, local_state, 0)

    def chain_copy():
        return remote(out_state, carry, misc_send.at[1], misc_recv.at[1], p.ring(1))

    turn_c, turn_s = math.cos(OMEGA * length), math.sin(OMEGA * length)

    def hand_on():
        def one(it, _):
            came = carry[it].astype(F32)
            came_c, came_s = came[:, 0:128], came[:, 128:256]
            turned = jnp.concatenate(
                [came_c * turn_c + came_s * turn_s, came_s * turn_c - came_c * turn_s], axis=1
            )
            state = out_state[it].astype(F32) + flags[it // pairs, 0:1, :] * turned
            out_state[it] = state.astype(BF16)
            return 0

        lax.fori_loop(0, total, one, 0)

    def chain_step():
        @pl.when(p.c == 0)
        def _():
            carry[...] = jnp.zeros_like(carry)

        @pl.when(p.c > 0)
        def _():
            chain_copy().wait_recv()
            hand_on()

        @pl.when(p.c < lay.C - 1)
        def _():
            chain_copy().start()

    pl.when(p.c == 0)(chain_step)
    project(q_out, 0, True)
    for copy in outputs[:3]:
        copy.start()
    pl.when(p.c == 1)(chain_step)
    go(2, ups[2:])
    step_block = 256 if length % 256 == 0 else length
    chain_turn = (total * 2) // 3 + ((p.c - 2) * (total // 3)) // max(lay.C - 2, 1)

    def local_attention(it, _):
        @pl.when((it == chain_turn) & (p.c > 1))
        def _():
            chain_step()

        for turn, number, some in ((3, 3, mixes), (5, 3, ups[:2]), (8, 1, downs)):

            @pl.when(it == (turn * total) // 12)
            def _(number=number, some=some):
                go(number, some)

        s, rows, lanes = where(it)
        low, high = lane_half(0), lane_half(1)
        queries, keys, values = q_out[rows, lanes], k_out[rows, lanes], v_out[rows, lanes]
        for b in range(length // step_block):
            lo, reach = b * step_block, (b + 1) * step_block
            q = queries[lo:reach]
            numer = jnp.zeros((step_block, 128), F32)
            denom = jnp.zeros((step_block, 128), F32)
            for side in (low, high):
                only = side.astype(BF16)
                scores = dot(q, keys[:reach] * only, NT) * mask[s, lo:reach, 0:reach]
                numer = numer + dot(scores.astype(BF16), values[:reach] * only)
                denom = denom + jnp.sum(scores, axis=1, keepdims=True) * side
            here = pl.ds(pl.multiple_of(s * length + lo, step_block), step_block)
            att[here, lanes] = numer
            den[here, lanes] = denom
        return 0

    lax.fori_loop(0, total, local_attention, 0)

    square = same_head()

    def finish(it, _):
        s, rows, lanes = where(it)
        state_c, state_s = unpack_state(carry[it])
        totals = []
        for part in (0, 1):
            line = carry[it, 64:80, part * 128 : part * 128 + 128].astype(F32)[0:1]
            totals.append(jnp.transpose(jnp.broadcast_to(line, (128, 128))) * square)
        wide = jnp.concatenate([state_c, state_s, totals[0], totals[1]], axis=1).astype(BF16)
        reach = dot(q_out[rows, lanes], wide)
        c_i, s_i = tab[s, 0], tab[s, 1]
        numer = att[rows, lanes] + c_i * reach[:, 0:128] + s_i * reach[:, 128:256]
        denom = den[rows, lanes] + c_i * reach[:, 256:384] + s_i * reach[:, 384:512]
        den[rows, lanes] = denom
        att[rows, lanes] = numer / jnp.maximum(denom, FLOOR)
        return 0

    lax.fori_loop(0, total, finish, 0)
    go(3, ups[2:])
    for number in () if split else (2, 3):
        go(number, downs)
    for flow in groups[1]:
        flow.arrive(3)
    unslot(g_mix, full_mix, lay, mix_s.shape[0], mix_s.shape[1], False)
    outputs[5].start()
    for flow in groups[2]:
        flow.arrive(3)
    for flow in groups[3]:
        flow.arrive(1 if split else 3)
    for flow in flows:
        flow.sent(range(2) if split and flow in groups[3] else range(4))
    ring_ids.wait_send()
    for copy in outputs:
        copy.wait()

    @pl.when(p.c < lay.C - 1)
    def _():
        chain_copy().wait_send()


def forward(lay, tokens, ids, bias, shards, split):
    seqs, length = ids.shape
    rows, width = tokens.shape
    total = seqs * (width // 128)
    cuts = [pieces(s.shape[0], n) for s, n in zip(shards, (3, 1, 2, 2), strict=True)]
    cuts = tuple(cuts)
    flows = sum(len(c) for c in cuts)
    vmem, anyspace = pl.BlockSpec(memory_space=pltpu.VMEM), pl.BlockSpec(memory_space=pl.ANY)
    slots = [(lay.X, 2, lay.Z, lay.Y) + s.shape for s in shards]
    shape = jax.ShapeDtypeStruct
    copied = [(rows, width)] * 3 + [(width, 3 * width), (width, width), (width, rows)]
    outs = (
        [shape((rows, width), F32)] * 2
        + [shape((total, 80, 256), BF16), shape(ids.shape, jnp.int32)]
        + [shape(s, BF16) for s in copied + slots[2:]]
    )
    return pl.pallas_call(
        functools.partial(forward_kernel, lay, seqs, length, cuts, split),
        out_shape=outs,
        in_specs=[vmem] * 7,
        out_specs=[vmem] * 4 + [anyspace] * 8,
        scratch_shapes=[pltpu.VMEM(s, BF16) for s in copied]
        + [
            pltpu.VMEM(slots[0], BF16),
            pltpu.VMEM(slots[1], BF16),
            pltpu.VMEM((1, 3 * width), F32),
            pltpu.VMEM((seqs, length, length), F32),
            pltpu.VMEM((seqs, 4, length, 128), F32),
                pltpu.VMEM((total, 80, 256), BF16),
            pltpu.VMEM((seqs, 8, 256), F32),
                pltpu.SemaphoreType.DMA((flows * lay.hops,)),
            pltpu.SemaphoreType.DMA((flows * lay.hops,)),
            pltpu.SemaphoreType.DMA((2,)),
            pltpu.SemaphoreType.DMA((2,)),
            pltpu.SemaphoreType.DMA((10,)),
        ],
        compiler_params=pltpu.CompilerParams(
            collective_id=0, has_side_effects=True, vmem_limit_bytes=VMEM_LIMIT
        ),
        name="forward_attention",
    )(tokens, ids, bias, *shards)


def normalize(values):
    center = values - jnp.mean(values, axis=-1, keepdims=True)
    scale = lax.rsqrt(jnp.mean(center * center, axis=-1, keepdims=True) + EPSILON)
    return center * scale, scale


def normalize_grad(grad, unit, scale):
    return (
        grad
        - jnp.mean(grad, axis=-1, keepdims=True)
        - unit * jnp.mean(grad * unit, axis=-1, keepdims=True)
    ) * scale


def rows_sum(values):
    return jnp.sum(values, axis=0, keepdims=True)


def dense_kernel(
    lay, row_blocks, chunk, split, gather_cuts, cuts, *refs
):
    tokens, att, den, cot = refs[:4]
    given_vectors = refs[4:11]
    w_mix_in, g_up, g_down = refs[11:14]
    layer_out, pre_out, given_out, d_mix, d_up, d_down_out, sums = refs[14:21]
    rest = refs[21:]
    if split:
        g_down, rest = rest[0], rest[1:]
    (w_mix, w_up, w_down, act, up_g, hid_t, down_t, att_t, mix_g, unit_v, scale_v, grad_v, vectors, acc, sem) = rest[:15]
    step = pl.program_id(0)
    block, width = tokens.shape
    ff = act.shape[1]
    mix_w, up_w = d_mix.shape[-1], d_up.shape[-1]
    down_a, down_w = g_down.shape[-2:] if split else d_down_out.shape[-2:]
    mix_b, down_b, gain1, shift1, gain2, shift2 = [vectors.at[i : i + 1, 0:width] for i in range(1, 7)]
    starts = [0, row_blocks, 2 * row_blocks, 2 * row_blocks + lay.Z, 3 * row_blocks + lay.Z]
    last_step = 3 * row_blocks + 2 * lay.Z - 1

    def fetch_mix():
        return [pltpu.make_async_copy(w_mix_in, w_mix, sem.at[0])]

    def fetch_up():
        if not split:
            return [pltpu.make_async_copy(g_up, w_up, sem.at[1])]
        return [
            pltpu.make_async_copy(g_up.at[c // 2, c % 2], w_up.at[:, :, :, pl.ds(c * up_w, up_w)], sem.at[3 + c])
            for c in range(lay.C)
        ]

    def fetch_down():
        if not split:
            return [pltpu.make_async_copy(g_down, w_down, sem.at[2])]
        return [
            pltpu.make_async_copy(
                g_down.at[c // 2, c % 2, r // lay.Y, r % lay.Y],
                w_down.at[c, :, pl.ds(r * down_w, down_w)],
                sem.at[3 + lay.C + c * lay.R + r],
            )
            for c in range(lay.C)
            for r in range(lay.R)
        ]

    if split:
        d_down, came, landing = rest[15], rest[16], rest[17:-4]
        send, recv, send2, recv2 = rest[-4:]
        p = Place(lay)
        gathers, scatters = [], []
        for n, (r0, size, y_first) in enumerate(gather_cuts):
            gathers.append(Gather(p, None, g_down, r0, size, y_first, send, recv, n * lay.hops))
        for n, (r0, size, y_first) in enumerate(cuts):
            scatters.append(
                Scatter(
                    p, d_down, d_down.at[:, p.k], came, landing[n], None, None, None,
                    r0, size, y_first, send2, recv2, n * lay.hops, None,
                )
            )
        out_copy = pltpu.make_async_copy(d_down.at[:, p.k], d_down_out, sem.at[1])

    wide = 2 * chunk if ff % (2 * chunk) == 0 else chunk

    @pl.when(step == 0)
    def _():
        for copy in fetch_mix() + fetch_up() + ([] if split else fetch_down()):
            copy.start()
        if split:
            p.barrier()
            for flow in gathers:
                flow.start(2)
        for i, vector in enumerate(given_vectors):
            vectors[i : i + 1, 0 : vector.shape[0]] = vector[...].astype(F32).reshape(1, vector.shape[0])
        acc[...] = jnp.zeros_like(acc)
        for copy in fetch_mix():
            copy.wait()

    @pl.when(step < starts[1])
    def _():
        rows = pl.ds(pl.multiple_of(step * block, block), block)
        att_low = att[...].astype(BF16)
        att_t[:, rows] = jnp.transpose(att_low)
        mixed = dot(att_low, w_mix[...]) + mix_b[...]
        unit1, scale1 = normalize(tokens[...].astype(F32) + mixed)
        unit_v[rows, :] = unit1
        scale_v[rows, :] = jnp.broadcast_to(scale1, (block, 128))
        hidden_low = (unit1 * gain1[...] + shift1[...]).astype(BF16)
        hid_t[:, rows] = jnp.transpose(hidden_low)

        @pl.when(step == 0)
        def _():
            for copy in fetch_up():
                copy.wait()

        def up_part(n, _):
            lanes = pl.ds(pl.multiple_of(n * wide, wide), wide)
            up = dot(hidden_low, w_up[:, :, :, lanes].reshape(width, wide)) + vectors[0:1, lanes]
            cdf = 0.5 + 0.5 * lax.erf(up * math.sqrt(0.5))
            density = jnp.exp(up * up * -0.5) * (1.0 / math.sqrt(2.0 * math.pi))
            up_g[rows, lanes] = (cdf + up * density).astype(BF16)
            act[rows, lanes] = (up * cdf).astype(BF16)
            if split:
                for turn, some in ((2, gathers[:2]), (3, gathers[2:])):

                    @pl.when((step == (turn * row_blocks) // 4) & (n == turn - 2))
                    def _(some=some):
                        for flow in some:
                            flow.advance(3)

            return 0

        lax.fori_loop(0, ff // wide, up_part, 0)

    if split:

        @pl.when(step == starts[1] - 1)
        def _():
            for flow in gathers:
                flow.arrive(3)
            for copy in fetch_down():
                copy.start()

    @pl.when(step == starts[1])
    def _():
        for copy in fetch_down():
            copy.wait()

    @pl.when((step >= starts[1]) & (step < starts[2]))
    def _():
        rows = pl.ds(pl.multiple_of((step - starts[1]) * block, block), block)

        down = dot(act[rows, :], w_down[...].reshape(width, ff), NT) + down_b[...]
        hidden = unit_v[rows, :] * gain1[...] + shift1[...]
        unit2, scale2 = normalize(hidden + down)
        layer_out[...] = (unit2 * gain2[...] + shift2[...]).astype(BF16)
        given = cot[...]
        acc[3:4, 0:width] += rows_sum(given * unit2)
        acc[3:4, width : 2 * width] += rows_sum(given)
        sum_grad = normalize_grad(given * gain2[...], unit2, scale2)
        grad_v[rows, :] = sum_grad
        down_grad = sum_grad.astype(BF16)
        down_t[:, rows] = jnp.transpose(down_grad)
        acc[2:3, 3 * width : 4 * width] += rows_sum(down_grad.astype(F32))

    @pl.when((step >= starts[2]) & (step < starts[3]))
    def _():
        n = step - starts[2]
        lanes = pl.ds(pl.multiple_of(n * chunk, chunk), chunk)
        part = dot(down_t[...], act[:, lanes]).astype(BF16)
        for c in range(lay.C):
            for y in range(lay.Y):
                tile = part[c * down_a : (c + 1) * down_a, y * down_w : (y + 1) * down_w]
                if split:
                    d_down[c // 2, c % 2, n, y] = tile
                else:
                    d_down_out[c // 2, c % 2, 0, y] = tile

    if split:

        @pl.when(step == starts[3])
        def _():
            for flow in scatters:
                flow.start(0)

        @pl.when(step == starts[3] + 1)
        def _():
            for flow in scatters:
                flow.advance(1)

        @pl.when(step == last_step)
        def _():
            for flow in scatters:
                flow.add(2)
            out_copy.start()
            for flow in gathers:
                flow.sent(range(2, 4))
            for flow in scatters:
                flow.sent(range(2))
            out_copy.wait()

    @pl.when((step >= starts[3]) & (step < starts[4]))
    def _():
        rows = pl.ds(pl.multiple_of((step - starts[3]) * block, block), block)
        sum_grad = grad_v[rows, :]
        down_grad = sum_grad.astype(BF16)

        def back(n, _):
            lanes = pl.ds(pl.multiple_of(n * wide, wide), wide)
            grad = dot(down_grad, w_down[:, :, lanes].reshape(width, wide)) * up_g[rows, lanes].astype(F32)
            grad = grad.astype(BF16)
            up_g[rows, lanes] = grad
            acc[0:1, lanes] += rows_sum(grad.astype(F32))
            return 0

        lax.fori_loop(0, ff // wide, back, 0)
        hidden_grad = sum_grad + dot(up_g[rows, :], w_up[...].reshape(width, ff), NT)
        unit1, scale1 = unit_v[rows, :], scale_v[rows, 0:1]
        acc[2:3, width : 2 * width] += rows_sum(hidden_grad * unit1)
        acc[2:3, 2 * width : 3 * width] += rows_sum(hidden_grad)
        pre_grad = normalize_grad(hidden_grad * gain1[...], unit1, scale1)
        pre_out[...] = pre_grad
        mixed_grad = pre_grad.astype(BF16)
        mix_g[rows, :] = mixed_grad
        acc[2:3, 0:width] += rows_sum(mixed_grad.astype(F32))
        att_grad = dot(mixed_grad, w_mix[...], NT)
        denom = den[...]
        inverse = 1.0 / jnp.maximum(denom, FLOOR)
        numer = att_grad * inverse
        weighted = att_grad * att[...]
        upper = weighted.astype(BF16)
        lower = (weighted - upper.astype(F32)).astype(BF16)
        square = same_head().astype(BF16)
        factor = inverse * (denom > FLOOR).astype(F32)
        lane = lax.broadcasted_iota(jnp.int32, (1, 128), 1)
        for t in range(width // 128):
            lanes = slice(t * 128, t * 128 + 128)
            summed = dot(upper[:, lanes], square) + dot(lower[:, lanes], square)
            extra = -summed * factor[:, lanes]
            extra = jnp.concatenate([extra[:, 64:128], extra[:, 0:64]], axis=1)
            extra_hi = extra.astype(BF16).astype(F32)
            for head in (0, 1):
                spare = 64 - 64 * head
                both = (
                    numer[:, lanes] * lane_half(head)
                    + extra_hi * (lane == spare).astype(F32)
                    + (extra - extra_hi) * (lane == spare + 1).astype(F32)
                )
                at = t * 256 + head * 128
                given_out[:, at : at + 128] = both.astype(BF16)

    @pl.when(step >= starts[4])
    def _():
        n = step - starts[4]
        lanes = pl.ds(pl.multiple_of(n * chunk, chunk), chunk)
        part = dot(hid_t[...], up_g[:, lanes]).astype(BF16)
        for i in range(chunk // up_w):
            d_up[i // 2, i % 2] = part[:, i * up_w : (i + 1) * up_w].reshape(d_up.shape[2:])

    @pl.when(step == starts[4])
    def _():
        part = dot(att_t[...], mix_g[...]).astype(BF16)
        for c in range(lay.C):
            d_mix[c // 2, c % 2] = part[:, c * mix_w : (c + 1) * mix_w].reshape(d_mix.shape[2:])
        sums[...] = acc[...]


def dense(lay, tokens, att, den, cot, vectors, w_mix, g_up, g_down, mix_shape, split):
    total, width = tokens.shape
    block = 256 if total % 256 == 0 else total
    row_blocks = total // block
    ff = g_up.shape[-1] * lay.C
    chunk = ff // lay.Z
    up_w = g_up.shape[-1]
    slots = [(lay.X, 2, lay.Z, lay.Y) + mix_shape, g_up.shape, g_down.shape]
    if not split:
        g_up = g_up.transpose(2, 3, 4, 0, 1, 5).reshape(lay.Z, lay.Y, g_up.shape[4], ff)
        g_down = g_down.transpose(0, 1, 4, 2, 3, 5).reshape(lay.C, g_down.shape[4], ff)
    starts = [0, row_blocks, 2 * row_blocks, 2 * row_blocks + lay.Z, 3 * row_blocks + lay.Z]
    last = row_blocks - 1
    per = chunk // up_w
    phase = lambda i, n, size: jnp.clip(i - starts[n], 0, size - 1)
    in_phase = lambda n, wide=width: pl.BlockSpec((block, wide), lambda i: (phase(i, n, row_blocks), 0))
    twice = pl.BlockSpec((block, width), lambda i: (jnp.where(i < starts[1], i, phase(i, 3, row_blocks)), 0))
    fixed = lambda shape: pl.BlockSpec(shape, lambda i: (0,) * len(shape), pipeline_mode=pl.Buffered(1))
    anyspace = pl.BlockSpec(memory_space=pl.ANY)
    later = lambda i: phase(i, 4, lay.Z)
    if per == 1:
        up_spec = pl.BlockSpec((1, 1) + slots[1][2:], lambda i: (later(i) // 2, later(i) % 2, 0, 0, 0, 0))
    else:
        up_spec = pl.BlockSpec((per // 2, 2) + slots[1][2:], lambda i: (later(i), 0, 0, 0, 0, 0))
    half = slots[2][:1] + slots[2][2:]
    gather_cuts, cuts = pieces(slots[2][4], 2), pieces(slots[2][4], 1)
    if split:
        down_shape, down_spec = half, anyspace
    else:
        down_shape = slots[2]
        down_spec = pl.BlockSpec(
            slots[2][:2] + (1,) + slots[2][3:], lambda i: (0, 0, phase(i, 2, lay.Z), 0, 0, 0)
        )
    shape = jax.ShapeDtypeStruct
    outs = [
        shape((total, width), BF16),
        shape((total, width), F32),
        shape((total, 2 * width), BF16),
        shape(slots[0], BF16),
        shape(slots[1], BF16),
        shape(down_shape, BF16),
        shape((4, ff), F32),
    ]
    out_specs = [
        in_phase(1), in_phase(3), in_phase(3, 2 * width), fixed(slots[0]), up_spec, down_spec, fixed((4, ff)),
    ]
    scratch = [
        pltpu.VMEM((width, width), BF16),
        pltpu.VMEM((lay.Z, lay.Y, slots[1][4], ff), BF16),
        pltpu.VMEM((lay.C, slots[2][4], ff), BF16),
        pltpu.VMEM((total, ff), BF16),
        pltpu.VMEM((total, ff), BF16),
        pltpu.VMEM((width, total), BF16),
        pltpu.VMEM((width, total), BF16),
        pltpu.VMEM((width, total), BF16),
        pltpu.VMEM((total, width), BF16),
        pltpu.VMEM((total, width), F32),
        pltpu.VMEM((total, 128), F32),
        pltpu.VMEM((total, width), F32),
        pltpu.VMEM((8, ff), F32),
        pltpu.VMEM((4, ff), F32),
        pltpu.SemaphoreType.DMA((3 + lay.C + lay.C * lay.R,)),
    ]
    params = dict(vmem_limit_bytes=VMEM_LIMIT)
    aliases = {}
    if split:
        outs.append(shape(slots[2], BF16))
        out_specs.append(anyspace)
        aliases = {13: 7}
        scratch += [pltpu.VMEM(slots[2], BF16), pltpu.VMEM(half, BF16)]
        for _, n, y_first in cuts:
            tile = (n, slots[2][5])
            first = (lay.Y - 1, lay.X, lay.Z) if y_first else (lay.X - 1, lay.Z, lay.Y)
            scratch.append(pltpu.VMEM(first + tile, BF16))
        for n in (gather_cuts, gather_cuts, cuts, cuts):
            scratch.append(pltpu.SemaphoreType.DMA((len(n) * lay.hops,)))
        params.update(collective_id=2, has_side_effects=True)
    results = pl.pallas_call(
        functools.partial(dense_kernel, lay, row_blocks, chunk, split, gather_cuts, cuts),
        grid=(3 * row_blocks + 2 * lay.Z,),
        out_shape=outs,
        in_specs=[in_phase(0), twice, in_phase(3), in_phase(1)] + [fixed(v.shape) for v in vectors] + [anyspace] * 3,
        out_specs=out_specs,
        scratch_shapes=scratch,
        input_output_aliases=aliases,
        compiler_params=pltpu.CompilerParams(**params),
        name="dense",
    )(tokens, att, den, cot, *vectors, w_mix, g_up, g_down)
    return results[:7]


class Scatter:
    def __init__(self, place, source, mine, came, second, third, fourth, target, r0, n, y_first, send, recv, base, fetch):
        self.p, self.source, self.mine, self.came = place, source, mine, came
        self.second, self.third, self.fourth, self.target = second, third, fourth, target
        self.rows, self.r0, self.n, self.y_first = pl.ds(r0, n), r0, n, y_first
        self.send, self.recv, self.base, self.fetch = send, recv, base, fetch

    def stage(self, number):
        p, rows, lay, mine = self.p, self.rows, self.p.lay, self.mine
        first, copies = self.base, []
        if number == 0:
            copies.append(
                (self.source.at[:, 1 - p.k, :, :, rows], self.came.at[:, :, :, rows], p.at(k=1 - p.k))
            )
        elif number == 3:
            first += 1 + lay.X - 1 + lay.Y - 1
            for d, z in enumerate(p.zs()):
                copies.append((mine.at[p.x, z, p.y, rows], self.fourth.at[d], p.at(z=z)))
        else:
            along_y = (number == 1) == self.y_first
            landing = self.second if number == 1 else self.third
            first += 1
            if number == 2:
                first += (lay.Y - 1) if self.y_first else (lay.X - 1)
            for d, other in enumerate(p.ys() if along_y else p.xs()):
                if along_y:
                    part = mine.at[:, :, other, rows] if number == 1 else mine.at[p.x, :, other, rows]
                    copies.append((part, landing.at[d], p.at(y=other)))
                else:
                    part = mine.at[other, :, :, rows] if number == 1 else mine.at[other, :, p.y, rows]
                    copies.append((part, landing.at[d], p.at(x=other)))
        return [
            remote(src, dst, self.send.at[first + i], self.recv.at[first + i], device)
            for i, (src, dst, device) in enumerate(copies)
        ]

    def own_copy(self):
        return pltpu.make_async_copy(
            self.source.at[:, self.p.k, :, :, self.rows], self.mine.at[:, :, :, self.rows], self.fetch
        )

    def start(self, number):
        for copy in self.stage(number):
            copy.start()

    def begin(self):
        self.start(0)
        if self.fetch is not None:
            self.own_copy().start()

    def advance(self, number):
        self.add(number)
        if number < 4:
            self.start(number)

    def add(self, number):
        p, rows, lay, mine = self.p, self.rows, self.p.lay, self.mine
        if number == 1 and self.fetch is not None:
            self.own_copy().wait()
        for copy in self.stage(number - 1):
            copy.wait_recv()
        if number == 1:

            def add(i, _):
                x, zy = i // (lay.Z * lay.Y), i % (lay.Z * lay.Y)
                z, y = zy // lay.Y, zy % lay.Y
                mine[x, z, y, rows] = (
                    mine[x, z, y, rows].astype(F32) + self.came[x, z, y, rows].astype(F32)
                ).astype(BF16)
                return 0

            lax.fori_loop(0, lay.X * lay.Z * lay.Y, add, 0)
        elif number == 2:
            outer = lay.X if self.y_first else lay.Z
            inner = lay.Z if self.y_first else lay.Y

            def add(i, _):
                a, b = i // inner, i % inner
                total = jnp.zeros((self.n, mine.shape[-1]), F32)
                for d in range(self.second.shape[0]):
                    total = total + self.second[d, a, b].astype(F32)
                if self.y_first:
                    mine[a, b, p.y, rows] = (mine[a, b, p.y, rows].astype(F32) + total).astype(BF16)
                else:
                    mine[p.x, a, b, rows] = (mine[p.x, a, b, rows].astype(F32) + total).astype(BF16)
                return 0

            lax.fori_loop(0, outer * inner, add, 0)
        elif number == 3:

            def add(z, _):
                total = mine[p.x, z, p.y, rows].astype(F32)
                for d in range(self.third.shape[0]):
                    total = total + self.third[d, z].astype(F32)
                mine[p.x, z, p.y, rows] = total.astype(BF16)
                return 0

            lax.fori_loop(0, lay.Z, add, 0)
        else:
            total = mine[p.x, p.z, p.y, rows].astype(F32)
            for d in range(lay.Z - 1):
                total = total + self.fourth[d].astype(F32)
            self.target[rows, :] = total

    def sent(self, numbers):
        for number in numbers:
            for copy in self.stage(number):
                copy.wait_send()


def backward_kernel(
    lay, seqs, length, cuts, split, *refs
):
    (carry, ids, prev, tok_t, sums, q_hbm, k_hbm, v_hbm, given_hbm, full_in, pre, d_mix, d_up, d_down) = refs[:14]
    (tokens_grad, o_in, o_mix, o_up, o_down, o_sums) = refs[14:20]
    rest = list(refs[20:])
    (mask, tab, out_state, in_state, flags, key_part, value_part, grads, held, given_in, d_in, vec, vec_in,
     mine_mix, mine_up, mine_down, came_mix, came_up, came_in) = rest[:19]
    send, recv, misc_send, misc_recv, local = rest[-5:]
    came_down = None if split else rest[19]
    landing = rest[19 if split else 20 : -5]
    p = Place(lay)
    total_rows, width = key_part.shape
    q_in, k_in, v_in = [held.at[:, pl.ds(i * width, width)] for i in range(3)]
    pairs = width // 128
    total = seqs * pairs
    spot = local.shape[0] - 4
    loads = [
        pltpu.make_async_copy(src, dst, local.at[spot + i])
        for i, (src, dst) in enumerate(((q_hbm, q_in), (k_hbm, k_in), (v_hbm, v_in), (given_hbm, given_in)))
    ]
    for copy in loads:
        copy.start()
    p.barrier()

    groups, base, used = [], 0, 0
    for index, (source, mine, came, target, parts) in enumerate(
        (
            (d_down, mine_down, came_down, o_down, cuts[0]),
            (d_up, mine_up, came_up, o_up, cuts[1]),
            (d_mix, mine_mix, came_mix, o_mix, cuts[2]),
            (d_in, d_in.at[:, p.k], came_in, o_in, cuts[3]),
        )
    ):
        group = []
        for r0, n, y_first in parts:
            second, third, fourth = landing[3 * used : 3 * used + 3]
            fetch = local.at[used] if index < 3 else None
            group.append(
                Scatter(p, source, mine, came, second, third, fourth, target, r0, n, y_first, send, recv, base, fetch)
            )
            base += lay.hops
            used += 1
        groups.append(group)
    if split:
        down_copy = pltpu.make_async_copy(d_down, mine_down, local.at[0])
        down_copy.start()
    for group in groups[1 if split else 0 : 3]:
        for flow in group:
            flow.begin()
    if split:
        down_copy.wait()
        for flow in groups[0]:
            flow.start(2)

    def pre_copy(b):
        return pltpu.make_async_copy(pre.at[pl.ds(b * 256, 256)], key_part.at[pl.ds(b * 256, 256)], misc_recv.at[2 + b])

    def grad_copy(b):
        return pltpu.make_async_copy(value_part.at[pl.ds(b * 256, 256)], tokens_grad.at[pl.ds(b * 256, 256)], misc_send.at[2 + b])

    blocks = total_rows // 256

    cos_a, sin_a, _, _ = angle_tables(length)
    cos_e, sin_e = edge_angles(cos_a, sin_a, length)
    for s in range(seqs):
        _, _, carried, last_mask, passes = seq_masks(ids, prev, s, length, p.c > 0)
        tab[s, 0] = cos_a * carried
        tab[s, 1] = sin_a * carried
        tab[s, 2] = cos_e * last_mask
        tab[s, 3] = sin_e * last_mask
        flags[s] = jnp.broadcast_to(passes, (8, 256))
    for copy in loads:
        copy.wait()

    def where(it):
        s, pair = it // pairs, it % pairs
        return s, pl.ds(pl.multiple_of(s * length, length), length), pl.ds(pl.multiple_of(pair * 128, 128), 128)

    def given_of(it):
        s, pair = it // pairs, it % pairs
        rows = pl.ds(pl.multiple_of(s * length, length), length)
        lane = lax.broadcasted_iota(jnp.int32, (1, 128), 1)
        plus = [given_in[rows, pl.ds(pl.multiple_of(pair * 256 + 128 * head, 128), 128)] for head in (0, 1)]
        given = plus[0] * lane_half(0).astype(BF16) + plus[1] * lane_half(1).astype(BF16)
        extra = jnp.zeros((length, 128), F32)
        for head in (0, 1):
            spare = 64 - 64 * head
            own = ((lane == spare) | (lane == spare + 1)).astype(F32)
            one = jnp.sum(plus[head].astype(F32) * own, axis=1, keepdims=True)
            extra = extra + one * lane_half(head)
        return plus, given, extra

    def local_state(it, _):
        s, rows, lanes = where(it)
        _, given, extra = given_of(it)
        queries, given = q_in[rows, lanes], given.astype(F32)
        scaled = jnp.concatenate([given * tab[s, 0], given * tab[s, 1]], axis=1).astype(BF16)
        state = dot(queries, scaled, TN)
        wide = queries.astype(F32) * extra
        for part in (0, 1):
            packed = pack_state(state[:, part * 128 : part * 128 + 128])
            out_state[it, 0:64, part * 128 : part * 128 + 128] = packed.astype(BF16)
            total_row = jnp.sum(wide * tab[s, part], axis=0, keepdims=True)
            out_state[it, 64:80, part * 128 : part * 128 + 128] = jnp.broadcast_to(total_row, (16, 128)).astype(BF16)
        return 0

    lax.fori_loop(0, total, local_state, 0)

    def chain_copy():
        return remote(out_state, in_state, misc_send.at[1], misc_recv.at[1], p.ring(-1))

    turn_c, turn_s = math.cos(OMEGA * length), math.sin(OMEGA * length)

    def hand_on():
        def one(it, _):
            came = in_state[it].astype(F32)
            came_c, came_s = came[:, 0:128], came[:, 128:256]
            turned = jnp.concatenate(
                [came_c * turn_c - came_s * turn_s, came_c * turn_s + came_s * turn_c], axis=1
            )
            state = out_state[it].astype(F32) + flags[it // pairs, 0:1, :] * turned
            out_state[it] = state.astype(BF16)
            return 0

        lax.fori_loop(0, total, one, 0)

    def chain_step():
        @pl.when(p.c == lay.C - 1)
        def _():
            in_state[...] = jnp.zeros_like(in_state)

        @pl.when(p.c < lay.C - 1)
        def _():
            chain_copy().wait_recv()
            hand_on()

        @pl.when(p.c > 0)
        def _():
            chain_copy().start()

    def onward(number, group):
        for flow in groups[group]:
            flow.advance(number)

    back = lay.C - 1 - p.c
    pl.when(back == 0)(chain_step)
    pl.when(back == 1)(chain_step)
    for group in (1, 2) if split else (0, 1):
        onward(1, group)
    chain_turn = (total * 2) // 3 + ((back - 2) * (total // 3)) // max(lay.C - 2, 1)

    during = [(1, 3, 0), (9, 2, 1), (10, 4, 0), (11, 2, 2)] if split else [(0, 1, 2), (3, 2, 0), (7, 2, 1), (9, 3, 0)]
    block = 256 if length % 256 == 0 else length

    def local_attention(it, _):
        @pl.when((it == chain_turn) & (back > 1))
        def _():
            chain_step()

        for turn, number, group in during:

            @pl.when(it == (turn * total) // 12)
            def _(number=number, group=group):
                onward(number, group)

        s, rows, lanes = where(it)
        for seq in range(seqs):

            @pl.when(it == seq * pairs)
            def _(seq=seq):
                row, column, _, _, _ = seq_masks(ids, prev, seq, length, p.c > 0)
                at_j = lax.broadcasted_iota(jnp.int32, (length, length), 0)
                at_i = lax.broadcasted_iota(jnp.int32, (length, length), 1)
                allowed = (column[:, 0:1] == row) & (at_j <= at_i)
                cos_a, sin_a, cos_r, sin_r = angle_tables(length)
                mask[...] = jnp.where(allowed, cos_a[:, 0:1] * cos_r + sin_a[:, 0:1] * sin_r, 0.0)

        lane = lax.broadcasted_iota(jnp.int32, (1, 128), 1)
        queries, keys, values = q_in[rows, lanes], k_in[rows, lanes], v_in[rows, lanes]
        plus, given, extra = given_of(it)
        query_total = jnp.zeros((length, 128), F32)
        for head in (0, 1):
            side = lane_half(head)
            only = side.astype(BF16)
            spare = 64 - 64 * head
            given_plus = plus[head]
            ones = ((lane == spare) | (lane == spare + 1)).astype(BF16)
            value_plus = values * only + ones
            key_only, query_only, given_only = keys * only, queries * only, given * only
            query_parts = []
            for b in range(length // block):
                lo = b * block
                scores = dot(key_only[lo : lo + block], queries[lo:], NT) * mask[lo : lo + block, lo:]
                grads_ji = (
                    dot(value_plus[lo : lo + block], given_plus[lo:], NT) * mask[lo : lo + block, lo:]
                ).astype(BF16)
                here = pl.ds(pl.multiple_of(s * length + lo, block), block)
                key_add = dot(grads_ji, query_only[lo:])
                value_add = dot(scores.astype(BF16), given_only[lo:])
                if head == 0:
                    key_part[here, lanes] = key_add
                    value_part[here, lanes] = value_add
                else:
                    key_part[here, lanes] += key_add
                    value_part[here, lanes] += value_add
                add = dot(grads_ji, key_only[lo : lo + block], TN)
                if lo:
                    query_total = jnp.concatenate([query_total[:lo], query_total[lo:] + add], axis=0)
                else:
                    query_total = query_total + add
        state_c, state_s = unpack_state(carry[it])
        wide = jnp.concatenate([state_c, state_s], axis=0).astype(BF16)
        reach = dot(given, wide, NT)
        totals = carry[it, 64:80, :].astype(F32)[0:1]
        query_total = query_total + tab[s, 0] * (reach[:, 0:128] + extra * totals[:, 0:128])
        query_total = query_total + tab[s, 1] * (reach[:, 128:256] + extra * totals[:, 128:256])
        grads[rows, lanes] = jnp.where(queries.astype(F32) > 0.0, query_total, 0.0).astype(BF16)
        return 0

    lax.fori_loop(0, total, local_attention, 0)

    def finish(it, _):
        s, rows, lanes = where(it)
        pair = it % pairs
        keys, values = k_in[rows, lanes], v_in[rows, lanes]
        state_c, state_s = unpack_state(in_state[it])
        by_row = jnp.concatenate([state_c, state_s], axis=0).astype(BF16)
        by_lane = jnp.concatenate([state_c, state_s], axis=1).astype(BF16)
        totals = in_state[it, 64:80, :].astype(F32)[0:1]
        c_j, s_j = tab[s, 2], tab[s, 3]
        key_reach = dot(values, by_row, NT) + totals
        value_reach = dot(keys, by_lane)
        key_grad = key_part[rows, lanes] + c_j * key_reach[:, 0:128] + s_j * key_reach[:, 128:256]
        value_grad = value_part[rows, lanes] + c_j * value_reach[:, 0:128] + s_j * value_reach[:, 128:256]
        key_lanes = pl.ds(pl.multiple_of(width + pair * 128, 128), 128)
        value_lanes = pl.ds(pl.multiple_of(2 * width + pair * 128, 128), 128)
        grads[rows, key_lanes] = jnp.where(keys.astype(F32) > 0.0, key_grad, 0.0).astype(BF16)
        grads[rows, value_lanes] = value_grad.astype(BF16)
        return 0

    lax.fori_loop(0, total, finish, 0)
    for number, group in [(3, 1), (3, 2)] if split else [(2, 2), (4, 0), (3, 1), (3, 2)]:
        onward(number, group)
    for b in range(blocks):
        pre_copy(b).start()
    weight_copy = pltpu.make_async_copy(full_in, held.at[pl.ds(0, width)], local.at[spot])
    weight_copy.start()
    vec[0] = sums[...]

    def bias_sum(n, _):
        lanes = pl.ds(pl.multiple_of(n * 256, 256), 256)
        vec[0, 1:2, lanes] = rows_sum(grads[:, lanes].astype(F32))
        return 0

    lax.fori_loop(0, 3 * width // 256, bias_sum, 0)

    in_a, in_w = o_in.shape
    piece = math.lcm(in_w, 128)

    def in_gradient(some):
        r0, n = some[0].r0, sum(flow.n for flow in some)
        left = jnp.concatenate([tok_t[r * in_a + r0 : r * in_a + r0 + n, :] for r in range(lay.R)], axis=0)
        for m in range(3 * width // piece):
            part = dot(left, grads[:, m * piece : (m + 1) * piece]).astype(BF16)
            for i in range(piece // in_w):
                c = m * (piece // in_w) + i
                tile = part[:, i * in_w : (i + 1) * in_w].reshape(lay.Z, lay.Y, n, in_w)
                d_in[c // 2, c % 2, :, :, r0 : r0 + n, :] = tile
        for flow in some:
            flow.begin()

    def vector_stage(number):
        first = (0, 1, lay.X, lay.X + lay.Y - 1)[number]
        peers = (
            [p.at(k=1 - p.k)],
            [p.at(x=x) for x in p.xs()],
            [p.at(y=y) for y in p.ys()],
            [p.at(z=z) for z in p.zs()],
        )[number]
        shift = 2 + blocks + first
        return [
            remote(vec.at[number], vec_in.at[first + i], misc_send.at[shift + i], misc_recv.at[shift + i], peer)
            for i, peer in enumerate(peers)
        ]

    def vector_start(number):
        for copy in vector_stage(number):
            copy.start()

    def vector_add(number):
        total_vec = vec[number]
        first = (0, 1, lay.X, lay.X + lay.Y - 1)[number]
        for i, copy in enumerate(vector_stage(number)):
            copy.wait_recv()
            total_vec = total_vec + vec_in[first + i]
        if number == 3:
            o_sums[...] = total_vec
        else:
            vec[number + 1] = total_vec
            vector_start(number + 1)

    def tokens_block(b):
        pre_copy(b).wait()
        part = slice(b * 256, (b + 1) * 256)
        value_part[part, :] = key_part[part, :] + dot(grads[part, :], held[0:width, :], NT)
        grad_copy(b).start()

    def go(number, some):
        for flow in some:
            flow.advance(number)

    ins = [groups[3][i : i + 2] for i in range(0, len(groups[3]), 2)]
    while len(ins) < 3:
        ins.append([])
    vector_start(0)
    for n in range(3):
        if ins[n]:
            in_gradient(ins[n])
        vector_add(n)
        if n:
            go(1, ins[n - 1])
    weight_copy.wait()
    tokens_block(0)
    go(1, ins[2])
    go(2, ins[0])
    vector_add(3)
    for b in range(1, blocks):
        tokens_block(b)
        if b == 1:
            go(2, ins[1])
    go(2, ins[2])
    go(3, ins[0])
    go(3, ins[1])
    go(3, ins[2])
    onward(4, 1)
    onward(4, 2)
    for some in ins:
        go(4, some)
    for b in range(blocks):
        grad_copy(b).wait()
    for group in groups:
        for flow in group:
            flow.sent(range(2, 4) if split and group is groups[0] else range(4))
    for number in range(4):
        for copy in vector_stage(number):
            copy.wait_send()

    @pl.when(p.c > 0)
    def _():
        chain_copy().wait_send()


def backward(
    lay, ids, prev, q, k, v, given, carry, tok_t, full_in, sums, pre, d_mix, d_up, d_down, shapes, split
):
    seqs, length = ids.shape
    rows, width = q.shape
    total = seqs * (width // 128)
    slots = [(lay.X, 2, lay.Z, lay.Y) + s for s in shapes]
    in_slots = slots[3]
    cuts = tuple(pieces(s[4], n) for s, n in zip(slots, (1, 1, 1, 3), strict=True))
    landing = []
    for index, (slot, parts) in enumerate(zip(slots, cuts, strict=True)):
        for _, n, y_first in parts:
            tile = (n, slot[5])
            if split and index == 0:
                landing += [(1, 1, 1, 16, 128), ((lay.X if y_first else lay.Y) - 1, lay.Z) + tile]
            elif y_first:
                landing += [(lay.Y - 1, lay.X, lay.Z) + tile, (lay.X - 1, lay.Z) + tile]
            else:
                landing += [(lay.X - 1, lay.Z, lay.Y) + tile, (lay.Y - 1, lay.Z) + tile]
            landing.append((lay.Z - 1,) + tile)
    flows = sum(len(c) for c in cuts)
    vmem, anyspace = pl.BlockSpec(memory_space=pltpu.VMEM), pl.BlockSpec(memory_space=pl.ANY)
    shape = jax.ShapeDtypeStruct
    ff = sums.shape[1]
    blocks = rows // 256
    half = [(s[0],) + s[2:] for s in slots]
    hop = lay.hops
    misc = 2 + blocks + hop
    scratch = [
        pltpu.VMEM((length, length), F32),
        pltpu.VMEM((seqs, 4, length, 128), F32),
        pltpu.VMEM((total, 80, 256), BF16),
        pltpu.VMEM((total, 80, 256), BF16),
        pltpu.VMEM((seqs, 8, 256), F32),
        pltpu.VMEM((rows, width), F32),
        pltpu.VMEM((rows, width), F32),
        pltpu.VMEM((rows, 3 * width), BF16),
        pltpu.VMEM((rows, 3 * width), BF16),
        pltpu.VMEM((rows, 2 * width), BF16),
        pltpu.VMEM(in_slots, BF16),
        pltpu.VMEM((4, 4, ff), F32),
        pltpu.VMEM((hop, 4, ff), F32),
    ]
    scratch += [pltpu.VMEM(half[i], BF16) for i in (2, 1, 0)] + [pltpu.VMEM(half[i], BF16) for i in ((2, 1, 3) if split else (2, 1, 3, 0))]
    scratch += [pltpu.VMEM(s, BF16) for s in landing]
    scratch += [
        pltpu.SemaphoreType.DMA((flows * hop,)),
        pltpu.SemaphoreType.DMA((flows * hop,)),
        pltpu.SemaphoreType.DMA((misc,)),
        pltpu.SemaphoreType.DMA((misc,)),
        pltpu.SemaphoreType.DMA((flows + 4,)),
    ]
    return pl.pallas_call(
        functools.partial(backward_kernel, lay, seqs, length, cuts, split),
        out_shape=[shape((rows, width), F32)]
        + [shape(slots[i][4:], F32) for i in (3, 2, 1, 0)]
        + [shape((4, ff), F32)],
        in_specs=[vmem] * 5 + [anyspace] * 9,
        out_specs=[anyspace] + [vmem] * 5,
        scratch_shapes=scratch,
        compiler_params=pltpu.CompilerParams(
            collective_id=1, has_side_effects=True, vmem_limit_bytes=VMEM_LIMIT
        ),
        name="backward_attention",
    )(carry, ids, prev, tok_t, sums, q, k, v, given, full_in, pre, d_mix, d_up, d_down)


def finish_kernel(tok_in, layer_in, in_in, mix_in, up_in, down_in, sums, *outs):
    layer_out, tokens_grad, o_in, in_b, o_mix, mix_b, gain1, shift1, o_up, up_b, o_down, down_b, gain2, shift2 = outs
    width = tok_in.shape[1]
    layer_out[...] = layer_in[...]
    tokens_grad[...] = tok_in[...]

    @pl.when(pl.program_id(0) == 0)
    def _():
        o_in[...] = in_in[...]
        o_mix[...] = mix_in[...]
        o_up[...] = up_in[...]
        o_down[...] = jnp.transpose(down_in[...])
        for out, row, at in (
            (up_b, 0, 0), (in_b, 1, 0), (mix_b, 2, 0), (gain1, 2, 1), (shift1, 2, 2), (down_b, 2, 3), (gain2, 3, 0), (shift2, 3, 1),
        ):
            size = out.shape[0]
            out[...] = sums[row : row + 1, at * width : at * width + size].reshape(size)


def finish_all(tokens_grad, layer_out, o_in, o_mix, o_up, o_down, sums):
    rows, width = tokens_grad.shape
    ff = sums.shape[1]
    block = 256 if rows % 256 == 0 else rows
    by_row = pl.BlockSpec((block, width), lambda i: (i, 0))
    fixed = lambda shape: pl.BlockSpec(shape, lambda i: (0,) * len(shape))
    sizes = [
        None, None, o_in.shape, (3 * width,), o_mix.shape, (width,), (width,), (width,), o_up.shape, (ff,),
        o_down.shape[::-1], (width,), (width,), (width,),
    ]
    shape = jax.ShapeDtypeStruct
    return pl.pallas_call(
        finish_kernel,
        grid=(rows // block,),
        out_shape=[shape((rows, width), BF16), shape((rows, width), F32)] + [shape(n, F32) for n in sizes[2:]],
        in_specs=[by_row] * 2 + [fixed(a.shape) for a in (o_in, o_mix, o_up, o_down, sums)],
        out_specs=[by_row] * 2 + [fixed(n) for n in sizes[2:]],
        name="finish",
    )(tokens_grad, layer_out, o_in, o_mix, o_up, o_down, sums)


def per_device(
    tokens, segment_ids, in_weight, in_bias, mix_weight, mix_bias, first_gain, first_shift,
    up_weight, up_bias, down_weight, down_bias, second_gain, second_shift, cotangent,
):
    lay = Layout(lax.axis_size("row"), lax.axis_size("col"))
    seqs, length, width = tokens.shape
    flat = tokens.reshape(seqs * length, width)
    split = up_weight.shape[1] % 128 == 0 and down_weight.shape[0] % 128 == 0
    shards = (in_weight, mix_weight, up_weight, down_weight.T)
    att, den, carry, prev, q, k, v, full_in, full_mix, tok_t, g_up, g_down = forward(
        lay, flat, segment_ids, in_bias, shards, split
    )
    vectors = (up_bias, mix_bias, down_bias, first_gain, first_shift, second_gain, second_shift)
    layer_out, pre, given, d_mix, d_up, d_down, sums = dense(
        lay, flat, att, den, cotangent.reshape(seqs * length, width), vectors, full_mix, g_up, g_down,
        mix_weight.shape, split,
    )
    tokens_grad, o_in, o_mix, o_up, o_down, o_sums = backward(
        lay, segment_ids, prev, q, k, v, given, carry, tok_t, full_in, sums, pre, d_mix, d_up, d_down,
        [shards[i].shape for i in (3, 2, 1, 0)], split,
    )
    outs = finish_all(tokens_grad, layer_out, o_in, o_mix, o_up, o_down, o_sums)
    return (outs[0].reshape(tokens.shape), outs[1].reshape(tokens.shape), *outs[2:])


def solution(mesh):
    block, matrix, rep = P("row", "col", None), P("row", "col"), P()
    return jax.shard_map(
        per_device,
        mesh=mesh,
        in_specs=(block, matrix, matrix, rep, matrix, rep, rep, rep, matrix, rep, matrix, rep, rep, rep, block),
        out_specs=(block, block, matrix, rep, matrix, rep, rep, rep, matrix, rep, matrix, rep, rep, rep),
        check_vma=False,
    )
```
